128 devices in a mesh: section: 8 (over x_lo, z), fsdp: 16 (over y, x_hi, core).
Axes of the slice: x: 4 (x_hi: 2, x_lo: 2; x = x_hi * 2 + x_lo), y: 4, z: 4, core: 2. Of those that a mesh axis runs over, the one named last changes fastest.
Arguments:
- feats: bfloat16 [4, 16, 256, 1536], P(None, 'fsdp'), may hold values from -6 to 6
- w_in: bfloat16 [2, 8, 1536, 3072], P(None, 'section', 'fsdp'), may hold values from -0.15625 to 0.15625
- dw_kernel: bfloat16 [2, 8, 31, 1536], P(None, 'section', None, 'fsdp'), may hold values from -1 to 1
- mask_embed: bfloat16 [1536], replicated, may hold values from -6 to 6
- w_ctx: bfloat16 [1536, 768], replicated, may hold values from -0.15625 to 0.15625
- w_tgt: bfloat16 [1536, 768], replicated, may hold values from -0.15625 to 0.15625
- mask_starts: int32 [4, 16, 12], P(None, 'fsdp'), may hold values from 0 to 246
- distractors: int32 [4, 16, 256, 100], P(None, 'fsdp', 'section'), may hold values from 0 to 255
Outputs:
- frame_loss: float32 [4, 16, 256], P(None, 'fsdp', 'section')
The draws below stay inside these ranges and needn't reach their ends.
All inputs are finite; a program needn't handle non-finite values.
Results may differ from the reference program's by a relative error of at most 0.0054.
Values may be sent and summed in bfloat16 or wider, within the bound.
A program may use at most 128 MiB of HBM per device.

```python
import jax
import jax.numpy as jnp
from jax import lax

D = 1536
E = 768
KERNEL = 31
NEG = 100
MASK_LEN = 10
SPANS = 12
MICRO = 4
REPEATS = 2
FRAMES = 256
SECTIONS = 8
UTTS = 16
N_SECTION = 8


def plant(array, stream_key, least, largest):
    index_at = [jax.random.randint(jax.random.fold_in(stream_key, axis), (), 0, length) for axis, length in enumerate(array.shape)]
    widest = array.shape.index(max(array.shape))
    next_to = index_at[:widest] + [(index_at[widest] + 1) % array.shape[widest]] + index_at[widest + 1:]
    return array.at[tuple(index_at)].set(least).at[tuple(next_to)].set(largest)


def block_levels(rng, shape, split, smallest, largest):
    level, own = 1.0, jax.random.fold_in(rng, 6)
    for dim, parts in split:
        steps = jnp.exp(jax.random.uniform(jax.random.fold_in(own, dim), (parts,), jnp.float32, smallest / len(split), largest / len(split)))
        level = level * jnp.repeat(steps, shape[dim] // parts).reshape([-1 if axis == dim else 1 for axis in range(len(shape))])
    return level


def centred(key, extent, deviation, bound, split=(), kind=jnp.bfloat16):
    drawn = jax.random.normal(key, extent, jnp.float32) * deviation
    if len(split) > 0:
        drawn = block_levels(key, extent, split, -0.22, 0.18) * drawn
    return jnp.clip(drawn, min=-bound, max=bound).astype(kind)


def setup_inputs(seed: int = 0) -> dict:
    key_of = jax.random.split(jax.random.key(seed), 9)
    feats = centred(key_of[0], (MICRO, UTTS, FRAMES, D), 1.0, 6.0, ((1, 16),))
    w_in = centred(key_of[1], (REPEATS, SECTIONS, D, 2 * D), D ** -0.5, 0.15625, ((1, 8), (2, 16)))
    dw_kernel = centred(key_of[2], (REPEATS, SECTIONS, KERNEL, D), KERNEL ** -0.5, 1.0, ((1, 8), (3, 16)))
    mask_embed = centred(key_of[3], (D,), 1.0, 6.0)
    w_ctx = centred(key_of[4], (D, E), D ** -0.5, 0.15625)
    w_tgt = centred(key_of[5], (D, E), D ** -0.5, 0.15625)
    mask_starts = plant(jax.random.randint(key_of[6], (MICRO, UTTS, SPANS), 0, FRAMES - MASK_LEN + 1), jax.random.fold_in(key_of[6], 1), 0, FRAMES - MASK_LEN).astype(jnp.int32)
    distractors = plant(jax.random.randint(key_of[7], (MICRO, UTTS, FRAMES, NEG), 0, FRAMES), jax.random.fold_in(key_of[7], 1), 0, FRAMES - 1).astype(jnp.int32)
    return dict(feats=feats, w_in=w_in, dw_kernel=dw_kernel, mask_embed=mask_embed, w_ctx=w_ctx, w_tgt=w_tgt, mask_starts=mask_starts, distractors=distractors)


def conv_layer(batch, weight, kernel):
    width = batch.shape[2]
    frames = batch.shape[1]
    values = batch.astype(jnp.float32)
    center = lax.optimization_barrier(jnp.mean(values, axis=2, keepdims=True))
    spread = lax.optimization_barrier(jnp.mean((values - center) ** 2, axis=2, keepdims=True))
    normed = ((values - center) * lax.rsqrt(spread + 1e-05)).astype(jnp.bfloat16)
    proj = jnp.dot(normed.reshape(-1, width), weight, preferred_element_type=jnp.float32)
    proj = proj.reshape(batch.shape[0], frames, 2 * width)
    glu = (proj[:, :, :width] * jax.nn.sigmoid(proj[:, :, width:])).astype(jnp.bfloat16)
    taps = kernel.shape[0]
    half = taps // 2
    padded = jnp.pad(glu, ((0, 0), (half, half), (0, 0)))
    mixed = jnp.zeros(values.shape, jnp.float32)
    for tap in range(taps):
        mixed = mixed + padded[:, tap:tap + frames, :].astype(jnp.float32) * kernel[tap].astype(jnp.float32)
    return (values + jax.nn.silu(mixed)).astype(jnp.bfloat16)

def unit_rows(values):
    return (values * lax.rsqrt(lax.optimization_barrier(jnp.sum(values * values, axis=-1, keepdims=True)) + 1e-06)).astype(jnp.bfloat16)

def reference(feats, w_in, dw_kernel, mask_embed, w_ctx, w_tgt, mask_starts, distractors):
    spots = jnp.arange(FRAMES, dtype=jnp.int32)
    starts = mask_starts[..., None]
    covered = jnp.any((spots >= starts) & (spots < starts + MASK_LEN), axis=2)
    masked = jnp.where(covered[..., None], mask_embed, feats)
    batch = masked.reshape(MICRO * UTTS, FRAMES, D)
    weights = w_in.reshape(REPEATS * N_SECTION, D, 2 * D)
    kernels = dw_kernel.reshape(REPEATS * N_SECTION, KERNEL, D)

    def layer_step(carry, pair):
        return (conv_layer(carry, pair[0], pair[1]), None)
    batch, unused = lax.scan(layer_step, batch, (weights, kernels))
    ctx = jnp.dot(batch.reshape(-1, D), w_ctx, preferred_element_type=jnp.float32)
    ctx = unit_rows(ctx).reshape(MICRO, UTTS, FRAMES, E)
    tgt = jnp.dot(feats.reshape(-1, D), w_tgt, preferred_element_type=jnp.float32)
    tgt = unit_rows(tgt).reshape(MICRO, UTTS, FRAMES, E)
    sims = jnp.einsum('mufe,muje->mufj', ctx.astype(jnp.float32), tgt.astype(jnp.float32))
    positive = jnp.diagonal(sims, axis1=2, axis2=3) * 10.0
    negative = jnp.take_along_axis(sims, distractors, axis=3) * 10.0
    total = jnp.exp(positive) + lax.optimization_barrier(jnp.sum(jnp.exp(negative), axis=3))
    return jnp.log(total) - positive
```

```python
import functools

import jax
import jax.numpy as jnp
from jax import lax
from jax.experimental import pallas as pl
from jax.experimental.pallas import tpu as pltpu
from jax.sharding import PartitionSpec as P

MASK_LEN = 10
TAPS = 31
CW = 256
LANES = 128
PAD = 16
GROUP = 64
MESH = pl.DeviceIdType.MESH


def relay_kernel(
    sections,
    x0_hbm,
    w_hbm,
    wctx_ref,
    tgt_ref,
    cnt_ref,
    out_ref,
    xin,
    xmid,
    obuf,
    nrm,
    gbuf,
    wv,
    kv,
    enc,
    cbuf,
    w_sem,
    x_sem,
    send_sem,
    recv_sem,
    csend_sem,
    crecv_sem,
):
    micro, chunks, frames, _ = xin.shape
    width = chunks * CW
    share = frames // sections
    s = lax.axis_index("section")
    last = sections - 1
    nxt = lax.rem(s + 1, sections)
    barrier = pltpu.get_barrier_semaphore()
    for j in range(sections):

        @pl.when(s != j)
        def _():
            pl.semaphore_signal(barrier, inc=1, device_id={"section": j}, device_id_type=MESH)

    pl.semaphore_wait(barrier, sections - 1)

    def load_w(layer):
        return pltpu.make_async_copy(w_hbm.at[layer], wv.at[layer], w_sem.at[layer])

    def load_x():
        return pltpu.make_async_copy(x0_hbm, xin, x_sem)

    load_w(0).start()

    @pl.when(s == 0)
    def _():
        load_x().start()

    load_w(1).start()

    for b in range(2):
        gbuf[b, 0:PAD, :] = jnp.zeros((PAD, LANES), jnp.float32)
        gbuf[b, PAD + frames : 2 * PAD + frames, :] = jnp.zeros((PAD, LANES), jnp.float32)

    def hop(i, c):
        return pltpu.make_async_remote_copy(
            src_ref=obuf.at[i, c],
            dst_ref=xin.at[i, c],
            send_sem=send_sem.at[i, c],
            recv_sem=recv_sem.at[i, c],
            device_id={"section": nxt},
            device_id_type=MESH,
        )

    def scatter(i, j):
        return pltpu.make_async_remote_copy(
            src_ref=cbuf.at[i, pl.ds(j * share, share)],
            dst_ref=enc.at[i],
            send_sem=csend_sem.at[i, j],
            recv_sem=crecv_sem.at[i],
            device_id={"section": j},
            device_id_type=MESH,
        )

    def taps_of(layer):
        for h in range(width // LANES):
            block = wv[layer, h * LANES : (h + 1) * LANES, 2 * width : 2 * width + LANES]
            kv[layer, h] = block.astype(jnp.float32).T[0:32, :]

    def normalise(x):
        total = jnp.zeros((frames, 1), jnp.float32)
        for c in range(chunks):
            total = total + jnp.sum(x[c].astype(jnp.float32), axis=1, keepdims=True)
        center = total / width
        total = jnp.zeros((frames, 1), jnp.float32)
        for c in range(chunks):
            off = x[c].astype(jnp.float32) - center
            total = total + jnp.sum(off * off, axis=1, keepdims=True)
        scale = lax.rsqrt(total / width + 1e-05)
        for c in range(chunks):
            off = x[c].astype(jnp.float32) - center
            nrm[:, c * CW : (c + 1) * CW] = (off * scale).astype(jnp.bfloat16)

    def chunk(layer, x, y, c):
        col = pl.multiple_of(c * CW, CW)
        gate_col = pl.multiple_of(width + c * CW, CW)
        value = jnp.dot(
            nrm[...], wv[layer, :, pl.ds(col, CW)], preferred_element_type=jnp.float32
        )
        gate = jnp.dot(
            nrm[...], wv[layer, :, pl.ds(gate_col, CW)], preferred_element_type=jnp.float32
        )
        glu = (value * jax.nn.sigmoid(gate)).astype(jnp.bfloat16).astype(jnp.float32)
        for h in range(CW // LANES):
            gbuf[h, PAD : PAD + frames, :] = glu[:, h * LANES : (h + 1) * LANES]
        for h in range(CW // LANES):
            for r in range(0, frames, GROUP):
                mixed = jnp.zeros((GROUP, LANES), jnp.float32)
                for k in range(TAPS):
                    taps = kv[layer, c * (CW // LANES) + h, k : k + 1, :]
                    mixed = mixed + gbuf[h, r + k + 1 : r + k + 1 + GROUP, :] * taps
                kept = x[c, r : r + GROUP, h * LANES : (h + 1) * LANES].astype(jnp.float32)
                y[c, r : r + GROUP, h * LANES : (h + 1) * LANES] = (
                    kept + mixed * jax.nn.sigmoid(mixed)
                ).astype(jnp.bfloat16)

    def one_micro(i, carry):
        @pl.when((i == 0) & (s == 0))
        def _():
            load_x().wait()

        @pl.when(s > 0)
        def _():
            for c in range(chunks):
                hop(i, c).wait_recv()

        normalise(xin.at[i])

        @pl.when(i == 0)
        def _():
            load_w(0).wait()
            taps_of(0)

        def chunk_a(c, carry):
            chunk(0, xin.at[i], xmid, c)
            return carry

        lax.fori_loop(0, chunks, chunk_a, 0)
        normalise(xmid)

        @pl.when(i == 0)
        def _():
            load_w(1).wait()
            taps_of(1)

        def chunk_b(c, carry):
            chunk(1, xmid, obuf.at[i], c)

            @pl.when(s < last)
            def _():
                hop(i, c).start()

            return carry

        lax.fori_loop(0, chunks, chunk_b, 0)

        @pl.when(s == last)
        def _():
            ctx = jnp.zeros((frames, wctx_ref.shape[1]), jnp.float32)
            for c in range(chunks):
                ctx = ctx + jnp.dot(
                    obuf[i, c],
                    wctx_ref[c * CW : (c + 1) * CW, :],
                    preferred_element_type=jnp.float32,
                )
            size = jnp.sum(ctx * ctx, axis=1, keepdims=True)
            cbuf[i] = (ctx * lax.rsqrt(size + 1e-06)).astype(jnp.bfloat16)
            for j in range(sections - 1):
                scatter(i, j).start()

        return carry

    lax.fori_loop(0, micro, one_micro, 0)

    @pl.when(s < last)
    def _():
        for i in range(micro):
            scatter(i, 0).wait_recv()

    @pl.when(s == last)
    def _():
        for i in range(micro):
            enc[i] = cbuf[i, last * share : (last + 1) * share, :]

    spots = lax.broadcasted_iota(jnp.int32, (share, frames), 1)
    rows = lax.broadcasted_iota(jnp.int32, (share, frames), 0) + s * share
    for i in range(micro):
        sims = 10.0 * lax.dot_general(
            enc[i], tgt_ref[i], (((1,), (1,)), ((), ())), preferred_element_type=jnp.float32
        )
        positive = jnp.sum(jnp.where(spots == rows, sims, 0.0), axis=1, keepdims=True)
        negative = jnp.sum(cnt_ref[i] * jnp.exp(sims), axis=1, keepdims=True)
        out_ref[i] = jnp.log(jnp.exp(positive) + negative) - positive

    @pl.when(s < last)
    def _():
        for i in range(micro):
            for c in range(chunks):
                hop(i, c).wait_send()

    @pl.when(s == last)
    def _():
        for i in range(micro):
            for j in range(sections - 1):
                scatter(i, j).wait_send()


def relay(sections, masked_in, weights, w_ctx, tgt, counts):
    micro, frames, width = masked_in.shape
    chunks = width // CW
    share = frames // sections
    proj = w_ctx.shape[1]
    x0 = masked_in.reshape(micro, frames, chunks, CW).transpose(0, 2, 1, 3)
    vmem = pl.BlockSpec(memory_space=pltpu.VMEM)
    hbm = pl.BlockSpec(memory_space=pl.ANY)
    return pl.pallas_call(
        functools.partial(relay_kernel, sections),
        out_shape=jax.ShapeDtypeStruct((micro, share, 1), jnp.float32),
        in_specs=[hbm, hbm, vmem, vmem, vmem],
        out_specs=vmem,
        scratch_shapes=[
            pltpu.VMEM((micro, chunks, frames, CW), jnp.bfloat16),
            pltpu.VMEM((chunks, frames, CW), jnp.bfloat16),
            pltpu.VMEM((micro, chunks, frames, CW), jnp.bfloat16),
            pltpu.VMEM((frames, width), jnp.bfloat16),
            pltpu.VMEM((CW // LANES, frames + 2 * PAD, LANES), jnp.float32),
            pltpu.VMEM(weights.shape, jnp.bfloat16),
            pltpu.VMEM((2, width // LANES, 32, LANES), jnp.float32),
            pltpu.VMEM((micro, share, proj), jnp.bfloat16),
            pltpu.VMEM((micro, frames, proj), jnp.bfloat16),
            pltpu.SemaphoreType.DMA((2,)),
            pltpu.SemaphoreType.DMA,
            pltpu.SemaphoreType.DMA((micro, chunks)),
            pltpu.SemaphoreType.DMA((micro, chunks)),
            pltpu.SemaphoreType.DMA((micro, sections)),
            pltpu.SemaphoreType.DMA((micro,)),
        ],
        compiler_params=pltpu.CompilerParams(
            collective_id=0, has_side_effects=True, vmem_limit_bytes=56 << 20
        ),
    )(x0, weights, w_ctx, tgt, counts)


def unit_rows(values):
    return (values * lax.rsqrt(jnp.sum(values * values, axis=-1, keepdims=True) + 1e-06)).astype(
        jnp.bfloat16
    )


def on_device(feats, w_in, dw_kernel, mask_embed, w_ctx, w_tgt, mask_starts, distractors):
    sections = lax.axis_size("section")
    section = lax.axis_index("section")
    frames = feats.shape[2]
    feats_local = feats[:, 0]
    half = sections // 2

    taps = dw_kernel[:, 0].transpose(0, 2, 1)
    taps = jnp.pad(taps, ((0, 0), (0, 0), (0, LANES - taps.shape[2])))
    rows = jnp.concatenate([w_in[:, 0], taps], axis=2)
    even = section % 2 == 0
    first = jnp.where(even, rows[0], rows[1])
    second = jnp.where(even, rows[1], rows[0])
    route_1 = [(i, i // 2 if i % 2 == 0 else half + i // 2) for i in range(sections)]
    route_2 = [(i, half + i // 2 if i % 2 == 0 else i // 2) for i in range(sections)]
    got_1 = lax.ppermute(first, "section", route_1)
    got_2 = lax.ppermute(second, "section", route_2)
    low = section < half
    pair = jnp.stack([jnp.where(low, got_1, got_2), jnp.where(low, got_2, got_1)])
    weights = lax.all_gather(pair, "fsdp", axis=1, tiled=True)

    spots = jnp.arange(frames, dtype=jnp.int32)
    starts = mask_starts[:, 0][:, :, None]
    covered = jnp.any(
        (spots[None, None, :] >= starts) & (spots[None, None, :] < starts + MASK_LEN), axis=1
    )
    masked_in = jnp.where(covered[:, :, None], mask_embed[None, None, :], feats_local)
    tgt = unit_rows(
        jnp.einsum("mjd,de->mje", feats_local, w_tgt, preferred_element_type=jnp.float32)
    )
    picks = distractors[:, 0]
    counts = jnp.sum((picks[..., None] == spots).astype(jnp.float32), axis=2)
    loss = relay(sections, masked_in, weights, w_ctx, tgt, counts)
    return loss[:, :, 0][:, None, :]


def solution(mesh):
    placed = (
        P(None, "fsdp", None, None),
        P(None, "section", "fsdp", None),
        P(None, "section", None, "fsdp"),
        P(),
        P(),
        P(),
        P(None, "fsdp", None),
        P(None, "fsdp", "section", None),
    )
    return jax.shard_map(
        on_device, mesh=mesh, in_specs=placed, out_specs=P(None, "fsdp", "section"), check_vma=False
    )
```

```python
import functools

import jax
import jax.numpy as jnp
from jax import lax
from jax.experimental import pallas as pl
from jax.experimental.pallas import tpu as pltpu
from jax.sharding import PartitionSpec as P

MASK_LEN = 10
TAPS = 31
CW = 256
LANES = 128
PAD = 16
GROUP = 64
CORES = 2
MESH = pl.DeviceIdType.MESH


def relay_kernel(
    sections,
    columns,
    feats_ref,
    wcat_ref,
    wctx_ref,
    wtgt_ref,
    embed_ref,
    starts_ref,
    picks_ref,
    out_ref,
    xin,
    xmid,
    obuf,
    pbuf,
    nrm,
    gbuf,
    wv,
    kv,
    tgt,
    cnt,
    enc,
    cbuf,
    own_send,
    own_recv,
    ring_send,
    ring_recv,
    init_send,
    init_recv,
    hop_send,
    hop_recv,
    fwd_send,
    fwd_recv,
    mid_send,
    mid_recv,
    fin_send,
    fin_recv,
    csend_sem,
    crecv_sem,
):
    utts, chunks, frames, _ = xin.shape
    micro = utts // CORES
    mine = chunks // CORES
    width = chunks * CW
    half = width // CORES
    share = frames // sections
    last = sections - 1
    rows = width // columns
    piece = rows * CORES
    s = lax.axis_index("section")
    f = lax.axis_index("fsdp")
    core = lax.rem(f, 2)
    peer = f + 1 - 2 * core
    x_hi = lax.rem(f // 2, 2)
    across = f + 2 - 4 * x_hi
    y = f // 4
    ys = columns // 4
    up = lax.rem(f + 4, columns)
    down = lax.rem(f + columns - 4, columns)
    nxt = lax.rem(s + 1, sections)

    barrier = pltpu.get_barrier_semaphore()
    for j in range(sections):

        @pl.when(s != j)
        def _():
            pl.semaphore_signal(
                barrier, inc=1, device_id={"section": j, "fsdp": f}, device_id_type=MESH
            )

        pl.semaphore_signal(
            barrier, inc=1, device_id={"section": j, "fsdp": peer}, device_id_type=MESH
        )
    for g in (up, down, across):
        pl.semaphore_signal(barrier, inc=1, device_id={"section": s, "fsdp": g}, device_id_type=MESH)
    pl.semaphore_wait(barrier, 2 * sections - 1 + 3)

    def remote(src, dst, send, recv, section, column):
        return pltpu.make_async_remote_copy(
            src_ref=src,
            dst_ref=dst,
            send_sem=send,
            recv_sem=recv,
            device_id={"section": section, "fsdp": column},
            device_id_type=MESH,
        )

    def rows_of(column):
        return pl.ds(pl.multiple_of(column * rows, 32), rows)

    def own_out(t, h):
        return remote(
            wcat_ref.at[t, h],
            wv.at[lax.rem(s, 2), rows_of(f)],
            own_send.at[t, h],
            own_recv.at[lax.rem(s, 2), core],
            s // 2 + (sections // 2) * t,
            f - core + h,
        )

    def own_here(t, h):
        return pltpu.make_async_copy(
            wcat_ref.at[t, h],
            wv.at[lax.rem(s, 2), rows_of(f)],
            own_recv.at[lax.rem(s, 2), core],
        )

    def own_in(a, c):
        return remote(
            wcat_ref.at[0, 0],
            wv.at[a, rows_of(f - core + c)],
            own_send.at[0, 0],
            own_recv.at[a, c],
            s,
            peer,
        )

    stays = [(s == 0), (s == last)]
    for t in range(2):
        for h in range(CORES):
            here = stays[t] & (core == h)

            @pl.when(here)
            def _():
                own_here(t, h).start()

            @pl.when(jnp.logical_not(here))
            def _():
                own_out(t, h).start()

    def part(y_at, x_at):
        chip = lax.rem(y_at + 2 * ys, ys) * 2 + x_at
        return pl.ds(pl.multiple_of(chip * piece, 64), piece)

    def ring(a, n, y_at, x_at, column):
        block = wv.at[a, part(y_at, x_at)]
        return remote(block, block, ring_send.at[a, n], ring_recv.at[a, n], s, column)

    other = 1 - x_hi

    def ring_out(a, n):
        y_at, x_at, column = (
            (y, x_hi, across),
            (y, x_hi, up),
            (y, x_hi, down),
            (y, other, up),
            (y, other, down),
            (y - 1, x_hi, up),
            (y + 1, other, down),
        )[n]
        return ring(a, n, y_at, x_at, column)

    def ring_in(a, n):
        y_at, x_at, column = (
            (y, other, across),
            (y - 1, x_hi, up),
            (y + 1, x_hi, down),
            (y - 1, other, up),
            (y + 1, other, down),
            (y - 2, x_hi, up),
            (y + 2, other, down),
        )[n]
        return ring(a, n, y_at, x_at, column)

    def gather_1(a):
        for c in range(CORES):
            t = a
            here = stays[t] & (core == c)

            @pl.when(here)
            def _():
                own_here(t, c).wait()

            @pl.when(jnp.logical_not(here))
            def _():
                own_in(a, c).wait_recv()

        for n in (0, 1, 2):
            ring_out(a, n).start()

    def gather_2(a):
        ring_in(a, 0).wait_recv()
        ring_out(a, 3).start()
        ring_out(a, 4).start()
        ring_in(a, 1).wait_recv()
        ring_out(a, 5).start()
        ring_in(a, 4).wait_recv()
        ring_out(a, 6).start()

    def gather_3(a):
        for n in (2, 3, 5, 6):
            ring_in(a, n).wait_recv()

    def init(m):
        at = xin.at[CORES * m + core]
        return remote(at, at, init_send.at[m], init_recv.at[m], s, peer)

    def init_in(m):
        at = xin.at[CORES * m + 1 - core]
        return remote(at, at, init_send.at[m], init_recv.at[m], s, peer)

    gather_1(0)

    @pl.when(s == 0)
    def _():
        spot = lax.broadcasted_iota(jnp.int32, (frames, CW), 0)

        def one(m, carry):
            covered = jnp.zeros((frames, CW), jnp.int32)
            for j in range(starts_ref.shape[1]):
                start = starts_ref[m, j]
                inside = (spot >= start) & (spot < start + MASK_LEN)
                covered = jnp.where(inside, 1, covered)
            for c in range(chunks):
                embed = embed_ref[:, c * CW : (c + 1) * CW].astype(jnp.float32)
                seen = feats_ref[m, :, c * CW : (c + 1) * CW].astype(jnp.float32)
                xin[CORES * m + core, c] = jnp.where(covered > 0, embed, seen).astype(jnp.bfloat16)
            init(m).start()
            return carry

        lax.fori_loop(0, micro, one, 0)

    def targets(m, carry):
        proj = jnp.dot(feats_ref[m], wtgt_ref[...], preferred_element_type=jnp.float32)
        size = jnp.sum(proj * proj, axis=1, keepdims=True)
        tgt[m] = (proj * lax.rsqrt(size + 1e-06)).astype(jnp.bfloat16)
        spots = lax.broadcasted_iota(jnp.int32, (share, frames), 1)
        total = jnp.zeros((share, frames), jnp.float32)
        for k in range(picks_ref.shape[2]):
            total = total + jnp.where(picks_ref[m, :, k : k + 1] == spots, 1.0, 0.0)
        cnt[m] = total
        return carry

    gather_2(0)
    gather_1(1)
    lax.fori_loop(0, micro, targets, 0)

    for b in range(CW // LANES):
        gbuf[b, 0:PAD, :] = jnp.zeros((PAD, LANES), jnp.float32)
        gbuf[b, PAD + frames : 2 * PAD + frames, :] = jnp.zeros((PAD, LANES), jnp.float32)

    gather_2(1)
    gather_3(0)

    def taps_of(a):
        for h in range(half // LANES):
            at = pl.ds(pl.multiple_of(core * half + h * LANES, LANES), LANES)
            block = wv[a, at, 2 * half : 2 * half + LANES]
            kv[a, h] = block.astype(jnp.float32).T[0:32, :]

    taps_of(0)

    def hop(i, j):
        return remote(
            obuf.at[i, j],
            xin.at[i, core * mine + j],
            hop_send.at[i, j],
            hop_recv.at[i, j],
            nxt,
            f,
        )

    def forward(i, j):
        at = xin.at[i, core * mine + j]
        return remote(at, at, fwd_send.at[i, j], fwd_recv.at[i, j], s, peer)

    def forward_in(i, j):
        at = xin.at[i, (1 - core) * mine + j]
        return remote(at, at, fwd_send.at[i, j], fwd_recv.at[i, j], s, peer)

    def middle(i, j):
        at = xmid.at[i, core * mine + j]
        return remote(at, at, mid_send.at[i, j], mid_recv.at[i, j], s, peer)

    def middle_in(i, j):
        at = xmid.at[i, (1 - core) * mine + j]
        return remote(at, at, mid_send.at[i, j], mid_recv.at[i, j], s, peer)

    def final(i, j):
        m = i // CORES
        return remote(obuf.at[i, j], pbuf.at[m, j], fin_send.at[m, j], fin_recv.at[m, j], s, peer)

    def scatter(m, j):
        return remote(
            cbuf.at[m, pl.ds(j * share, share)],
            enc.at[m],
            csend_sem.at[m, j],
            crecv_sem.at[m],
            j,
            f,
        )

    def normalise(x):
        total = jnp.zeros((frames, 1), jnp.float32)
        for c in range(chunks):
            total = total + jnp.sum(x[c].astype(jnp.float32), axis=1, keepdims=True)
        center = total / width
        total = jnp.zeros((frames, 1), jnp.float32)
        for c in range(chunks):
            off = x[c].astype(jnp.float32) - center
            total = total + jnp.sum(off * off, axis=1, keepdims=True)
        scale = lax.rsqrt(total / width + 1e-05)
        for c in range(chunks):
            off = x[c].astype(jnp.float32) - center
            nrm[:, c * CW : (c + 1) * CW] = (off * scale).astype(jnp.bfloat16)

    def chunk(a, x, y, j):
        col = pl.multiple_of(j * CW, CW)
        gate_col = pl.multiple_of(half + j * CW, CW)
        value = jnp.dot(nrm[...], wv[a, :, pl.ds(col, CW)], preferred_element_type=jnp.float32)
        gate = jnp.dot(nrm[...], wv[a, :, pl.ds(gate_col, CW)], preferred_element_type=jnp.float32)
        glu = (value * jax.nn.sigmoid(gate)).astype(jnp.bfloat16).astype(jnp.float32)
        for h in range(CW // LANES):
            gbuf[h, PAD : PAD + frames, :] = glu[:, h * LANES : (h + 1) * LANES]
        for h in range(CW // LANES):
            lane = slice(h * LANES, (h + 1) * LANES)
            for r in range(0, frames, GROUP):
                mixed = jnp.zeros((GROUP, LANES), jnp.float32)
                for k in range(TAPS):
                    taps = kv[a, j * (CW // LANES) + h, k : k + 1, :]
                    mixed = mixed + gbuf[h, r + k + 1 : r + k + 1 + GROUP, :] * taps
                kept = x[r : r + GROUP, lane].astype(jnp.float32)
                y[r : r + GROUP, lane] = (kept + mixed * jax.nn.sigmoid(mixed)).astype(jnp.bfloat16)

    def one_utt(i, carry):
        m = i // CORES
        ours = lax.rem(i, CORES) == core

        @pl.when((s == 0) & jnp.logical_not(ours))
        def _():
            init_in(m).wait_recv()

        @pl.when(s > 0)
        def _():
            for j in range(mine):
                hop(i, j).wait_recv()
                forward(i, j).start()
            for j in range(mine):
                forward_in(i, j).wait_recv()

        normalise(xin.at[i])

        def chunk_a(j, carry):
            at = core * mine + j
            chunk(0, xin.at[i, at], xmid.at[i, at], j)
            middle(i, j).start()
            return carry

        lax.fori_loop(0, mine, chunk_a, 0)

        @pl.when(i == 0)
        def _():
            gather_3(1)
            taps_of(1)

        for j in range(mine):
            middle_in(i, j).wait_recv()
        normalise(xmid.at[i])

        def chunk_b(j, carry):
            at = core * mine + j
            chunk(1, xmid.at[i, at], obuf.at[i, j], j)

            @pl.when(s < last)
            def _():
                hop(i, j).start()

            @pl.when((s == last) & jnp.logical_not(ours))
            def _():
                final(i, j).start()

            return carry

        lax.fori_loop(0, mine, chunk_b, 0)

        @pl.when((s == last) & ours)
        def _():
            ctx = jnp.zeros((frames, wctx_ref.shape[1]), jnp.float32)
            for j in range(mine):
                at = pl.ds(pl.multiple_of((core * mine + j) * CW, CW), CW)
                ctx = ctx + jnp.dot(obuf[i, j], wctx_ref[at, :], preferred_element_type=jnp.float32)
            for j in range(mine):
                final(i, j).wait_recv()
                at = pl.ds(pl.multiple_of(((1 - core) * mine + j) * CW, CW), CW)
                ctx = ctx + jnp.dot(pbuf[m, j], wctx_ref[at, :], preferred_element_type=jnp.float32)
            size = jnp.sum(ctx * ctx, axis=1, keepdims=True)
            cbuf[m] = (ctx * lax.rsqrt(size + 1e-06)).astype(jnp.bfloat16)
            for j in range(sections - 1):
                scatter(m, j).start()

        return carry

    lax.fori_loop(0, utts, one_utt, 0)

    def score(m, carry):
        @pl.when(s < last)
        def _():
            scatter(m, 0).wait_recv()

        @pl.when(s == last)
        def _():
            enc[m] = cbuf[m, last * share : (last + 1) * share, :]

        spots = lax.broadcasted_iota(jnp.int32, (share, frames), 1)
        rows_at = lax.broadcasted_iota(jnp.int32, (share, frames), 0) + s * share
        sims = 10.0 * lax.dot_general(
            enc[m], tgt[m], (((1,), (1,)), ((), ())), preferred_element_type=jnp.float32
        )
        positive = jnp.sum(jnp.where(spots == rows_at, sims, 0.0), axis=1, keepdims=True)
        negative = jnp.sum(cnt[m] * jnp.exp(sims), axis=1, keepdims=True)
        out_ref[m] = jnp.log(jnp.exp(positive) + negative) - positive
        return carry

    lax.fori_loop(0, micro, score, 0)

    for t in range(2):
        for h in range(CORES):

            @pl.when(jnp.logical_not(stays[t] & (core == h)))
            def _():
                own_out(t, h).wait_send()

    for a in range(2):
        for n in range(7):
            ring_out(a, n).wait_send()

    @pl.when(s == 0)
    def _():
        for m in range(micro):
            init(m).wait_send()

    def drain(i, carry):
        for j in range(mine):
            middle(i, j).wait_send()

            @pl.when(s < last)
            def _():
                hop(i, j).wait_send()

            @pl.when(s > 0)
            def _():
                forward(i, j).wait_send()

            @pl.when((s == last) & (lax.rem(i, CORES) != core))
            def _():
                final(i, j).wait_send()

        return carry

    lax.fori_loop(0, utts, drain, 0)

    @pl.when(s == last)
    def _():
        for m in range(micro):
            for j in range(sections - 1):
                scatter(m, j).wait_send()


def relay(sections, columns, feats, wcat, w_ctx, w_tgt, embed, starts, picks):
    micro, frames, width = feats.shape
    chunks = width // CW
    share = frames // sections
    proj = w_ctx.shape[1]
    utts = CORES * micro
    mine = chunks // CORES
    half = width // CORES
    vmem = pl.BlockSpec(memory_space=pltpu.VMEM)
    smem = pl.BlockSpec(memory_space=pltpu.SMEM)
    dma = pltpu.SemaphoreType.DMA
    bf16 = jnp.bfloat16
    return pl.pallas_call(
        functools.partial(relay_kernel, sections, columns),
        out_shape=jax.ShapeDtypeStruct((micro, share, 1), jnp.float32),
        in_specs=[vmem, vmem, vmem, vmem, vmem, smem, vmem],
        out_specs=vmem,
        scratch_shapes=[
            pltpu.VMEM((utts, chunks, frames, CW), bf16),
            pltpu.VMEM((utts, chunks, frames, CW), bf16),
            pltpu.VMEM((utts, mine, frames, CW), bf16),
            pltpu.VMEM((micro, mine, frames, CW), bf16),
            pltpu.VMEM((frames, width), bf16),
            pltpu.VMEM((CW // LANES, frames + 2 * PAD, LANES), jnp.float32),
            pltpu.VMEM((2, width, wcat.shape[3]), bf16),
            pltpu.VMEM((2, half // LANES, 32, LANES), jnp.float32),
            pltpu.VMEM((micro, frames, proj), bf16),
            pltpu.VMEM((micro, share, frames), jnp.float32),
            pltpu.VMEM((micro, share, proj), bf16),
            pltpu.VMEM((micro, frames, proj), bf16),
            dma((2, CORES)),
            dma((2, CORES)),
            dma((2, 7)),
            dma((2, 7)),
            dma((micro,)),
            dma((micro,)),
            dma((utts, mine)),
            dma((utts, mine)),
            dma((utts, mine)),
            dma((utts, mine)),
            dma((utts, mine)),
            dma((utts, mine)),
            dma((micro, mine)),
            dma((micro, mine)),
            dma((micro, sections)),
            dma((micro,)),
        ],
        compiler_params=pltpu.CompilerParams(
            collective_id=0, has_side_effects=True, vmem_limit_bytes=60 << 20
        ),
    )(feats, wcat, w_ctx, w_tgt, embed, starts, picks)


def on_device(feats, w_in, dw_kernel, mask_embed, w_ctx, w_tgt, mask_starts, distractors):
    sections = lax.axis_size("section")
    columns = lax.axis_size("fsdp")
    width = feats.shape[3]
    half = width // CORES

    taps = dw_kernel[:, 0].transpose(0, 2, 1)
    taps = jnp.pad(taps, ((0, 0), (0, 0), (0, LANES - taps.shape[2])))
    rows = w_in[:, 0]
    wcat = jnp.stack(
        [
            jnp.concatenate(
                [
                    rows[:, :, h * half : (h + 1) * half],
                    rows[:, :, width + h * half : width + (h + 1) * half],
                    taps,
                ],
                axis=2,
            )
            for h in range(CORES)
        ],
        axis=1,
    )
    loss = relay(
        sections,
        columns,
        feats[:, 0],
        wcat,
        w_ctx,
        w_tgt,
        mask_embed[None, :],
        mask_starts[:, 0],
        distractors[:, 0],
    )
    return loss[:, :, 0][:, None, :]


def solution(mesh):
    placed = (
        P(None, "fsdp", None, None),
        P(None, "section", "fsdp", None),
        P(None, "section", None, "fsdp"),
        P(),
        P(),
        P(),
        P(None, "fsdp", None),
        P(None, "fsdp", "section", None),
    )
    return jax.shard_map(
        on_device, mesh=mesh, in_specs=placed, out_specs=P(None, "fsdp", "section"), check_vma=False
    )
```

```python
import functools

import jax
import jax.numpy as jnp
from jax import lax
from jax.experimental import pallas as pl
from jax.experimental.pallas import tpu as pltpu
from jax.sharding import PartitionSpec as P

MASK_LEN = 10
TAPS = 31
LANES = 128
PAD = 16
GROUP = 32
CORES = 2
MESH = pl.DeviceIdType.MESH


def relay_kernel(
    sections,
    columns,
    feats_ref,
    wcat_ref,
    wctx_ref,
    wtgt_ref,
    embed_ref,
    starts_ref,
    picks_ref,
    out_ref,
    xin,
    xmid,
    obuf,
    pbuf,
    nrm,
    gbuf_0,
    gbuf_1,
    wv,
    kv,
    tgt,
    cnt,
    enc,
    cbuf,
    own_send,
    own_recv,
    ring_send,
    ring_recv,
    init_send,
    init_recv,
    hop_send,
    hop_recv,
    fwd_send,
    fwd_recv,
    mid_send,
    mid_recv,
    fin_send,
    fin_recv,
    csend_sem,
    crecv_sem,
):
    utts, chunks, frames, _ = xin.shape
    micro = utts // CORES
    mine = chunks // CORES
    width = chunks * LANES
    half = width // CORES
    share = frames // sections
    last = sections - 1
    rows = width // columns
    piece = rows * CORES
    s = lax.axis_index("section")
    f = lax.axis_index("fsdp")
    core = lax.rem(f, 2)
    peer = f + 1 - 2 * core
    x_hi = lax.rem(f // 2, 2)
    across = f + 2 - 4 * x_hi
    y = f // 4
    ys = columns // 4
    up = lax.rem(f + 4, columns)
    down = lax.rem(f + columns - 4, columns)
    nxt = lax.rem(s + 1, sections)

    barrier = pltpu.get_barrier_semaphore()
    for j in range(sections):

        @pl.when(s != j)
        def _():
            pl.semaphore_signal(
                barrier, inc=1, device_id={"section": j, "fsdp": f}, device_id_type=MESH
            )

        pl.semaphore_signal(
            barrier, inc=1, device_id={"section": j, "fsdp": peer}, device_id_type=MESH
        )
    for g in (up, down, across):
        pl.semaphore_signal(barrier, inc=1, device_id={"section": s, "fsdp": g}, device_id_type=MESH)
    pl.semaphore_wait(barrier, 2 * sections - 1 + 3)

    def remote(src, dst, send, recv, section, column):
        return pltpu.make_async_remote_copy(
            src_ref=src,
            dst_ref=dst,
            send_sem=send,
            recv_sem=recv,
            device_id={"section": section, "fsdp": column},
            device_id_type=MESH,
        )

    def rows_of(column):
        return pl.ds(pl.multiple_of(column * rows, 32), rows)

    def own_out(t, h):
        return remote(
            wcat_ref.at[t, h],
            wv.at[lax.rem(s, 2), rows_of(f)],
            own_send.at[t, h],
            own_recv.at[lax.rem(s, 2), core],
            s // 2 + (sections // 2) * t,
            f - core + h,
        )

    def own_here(t, h):
        return pltpu.make_async_copy(
            wcat_ref.at[t, h],
            wv.at[lax.rem(s, 2), rows_of(f)],
            own_recv.at[lax.rem(s, 2), core],
        )

    def own_in(a, c):
        return remote(
            wcat_ref.at[0, 0],
            wv.at[a, rows_of(f - core + c)],
            own_send.at[0, 0],
            own_recv.at[a, c],
            s,
            peer,
        )

    stays = [(s == 0), (s == last)]

    def send_own(t):
        for h in range(CORES):
            here = stays[t] & (core == h)

            @pl.when(here)
            def _():
                own_here(t, h).start()

            @pl.when(jnp.logical_not(here))
            def _():
                own_out(t, h).start()

    low = s < sections // 2
    send_own(0)

    @pl.when(jnp.logical_not(low))
    def _():
        send_own(1)

    def part(y_at, x_at):
        chip = lax.rem(y_at + 2 * ys, ys) * 2 + x_at
        return pl.ds(pl.multiple_of(chip * piece, 64), piece)

    def ring(a, n, y_at, x_at, column):
        block = wv.at[a, part(y_at, x_at)]
        return remote(block, block, ring_send.at[a, n], ring_recv.at[a, n], s, column)

    other = 1 - x_hi

    def ring_out(a, n):
        y_at, x_at, column = (
            (y, x_hi, across),
            (y, x_hi, up),
            (y, x_hi, down),
            (y, other, up),
            (y, other, down),
            (y - 1, x_hi, up),
            (y + 1, other, down),
        )[n]
        return ring(a, n, y_at, x_at, column)

    def ring_in(a, n):
        y_at, x_at, column = (
            (y, other, across),
            (y - 1, x_hi, up),
            (y + 1, x_hi, down),
            (y - 1, other, up),
            (y + 1, other, down),
            (y - 2, x_hi, up),
            (y + 2, other, down),
        )[n]
        return ring(a, n, y_at, x_at, column)

    def gather_1(a):
        for c in range(CORES):
            t = a
            here = stays[t] & (core == c)

            @pl.when(here)
            def _():
                own_here(t, c).wait()

            @pl.when(jnp.logical_not(here))
            def _():
                own_in(a, c).wait_recv()

        for n in (0, 1, 2):
            ring_out(a, n).start()

    def gather_2(a):
        ring_in(a, 0).wait_recv()
        ring_out(a, 3).start()
        ring_out(a, 4).start()
        ring_in(a, 1).wait_recv()
        ring_out(a, 5).start()
        ring_in(a, 4).wait_recv()
        ring_out(a, 6).start()

    def gather_3(a):
        for n in (2, 3, 5, 6):
            ring_in(a, n).wait_recv()

    def init(m):
        at = xin.at[CORES * m + core]
        return remote(at, at, init_send.at[m], init_recv.at[m], s, peer)

    def init_in(m):
        at = xin.at[CORES * m + 1 - core]
        return remote(at, at, init_send.at[m], init_recv.at[m], s, peer)

    gather_1(0)

    @pl.when(s == 0)
    def _():
        spot = lax.broadcasted_iota(jnp.int32, (frames, LANES), 0)

        def one(m, carry):
            covered = jnp.zeros((frames, LANES), jnp.int32)
            for j in range(starts_ref.shape[1]):
                start = starts_ref[m, j]
                inside = (spot >= start) & (spot < start + MASK_LEN)
                covered = jnp.where(inside, 1, covered)
            for c in range(chunks):
                embed = embed_ref[:, c * LANES : (c + 1) * LANES].astype(jnp.float32)
                seen = feats_ref[m, :, c * LANES : (c + 1) * LANES].astype(jnp.float32)
                xin[CORES * m + core, c] = jnp.where(covered > 0, embed, seen).astype(jnp.bfloat16)
            init(m).start()
            return carry

        lax.fori_loop(0, micro, one, 0)

    def targets(m, carry):
        proj = jnp.dot(feats_ref[m], wtgt_ref[...], preferred_element_type=jnp.float32)
        size = jnp.sum(proj * proj, axis=1, keepdims=True)
        tgt[m] = (proj * lax.rsqrt(size + 1e-06)).astype(jnp.bfloat16)
        spots = lax.broadcasted_iota(jnp.int32, (share, frames), 1)
        total = jnp.zeros((share, frames), jnp.float32)
        for k in range(picks_ref.shape[2]):
            total = total + jnp.where(picks_ref[m, :, k : k + 1] == spots, 1.0, 0.0)
        cnt[m] = total
        return carry

    lax.fori_loop(0, micro, targets, 0)
    gather_2(0)

    gather_1(1)

    @pl.when(low)
    def _():
        send_own(1)


    for g in (gbuf_0, gbuf_1):
        g[0:PAD, :] = jnp.zeros((PAD, LANES), jnp.float32)
        g[PAD + frames : 2 * PAD + frames, :] = jnp.zeros((PAD, LANES), jnp.float32)

    gather_2(1)
    gather_3(0)

    def taps_of(a):
        for h in range(half // LANES):
            at = pl.ds(pl.multiple_of(core * half + h * LANES, LANES), LANES)
            block = wv[a, at, 2 * half : 2 * half + LANES]
            kv[a, h] = block.astype(jnp.float32).T[0:32, :]

    taps_of(0)

    def hop(i, j):
        return remote(
            obuf.at[i, j],
            xin.at[i, core * mine + j],
            hop_send.at[i, j],
            hop_recv.at[i, j],
            nxt,
            f,
        )

    def forward(i, j):
        at = xin.at[i, core * mine + j]
        return remote(at, at, fwd_send.at[i, j], fwd_recv.at[i, j], s, peer)

    def forward_in(i, j):
        at = xin.at[i, (1 - core) * mine + j]
        return remote(at, at, fwd_send.at[i, j], fwd_recv.at[i, j], s, peer)

    def middle(i, j):
        at = xmid.at[i, core * mine + j]
        return remote(at, at, mid_send.at[i, j], mid_recv.at[i, j], s, peer)

    def middle_in(i, j):
        at = xmid.at[i, (1 - core) * mine + j]
        return remote(at, at, mid_send.at[i, j], mid_recv.at[i, j], s, peer)

    def final(i, j):
        m = i // CORES
        return remote(obuf.at[i, j], pbuf.at[m, j], fin_send.at[m, j], fin_recv.at[m, j], s, peer)

    def scatter(m, j):
        return remote(
            cbuf.at[m, pl.ds(j * share, share)],
            enc.at[m],
            csend_sem.at[m, j],
            crecv_sem.at[m],
            j,
            f,
        )

    def normalise(x):
        total = jnp.zeros((frames, 1), jnp.float32)
        for c in range(chunks):
            total = total + jnp.sum(x[c].astype(jnp.float32), axis=1, keepdims=True)
        center = total / width
        total = jnp.zeros((frames, 1), jnp.float32)
        for c in range(chunks):
            off = x[c].astype(jnp.float32) - center
            total = total + jnp.sum(off * off, axis=1, keepdims=True)
        scale = lax.rsqrt(total / width + 1e-05)
        for c in range(chunks):
            off = x[c].astype(jnp.float32) - center
            nrm[:, c * LANES : (c + 1) * LANES] = (off * scale).astype(jnp.bfloat16)

    def chunk(a, x, y, j):
        g = (gbuf_0, gbuf_1)[j % 2]
        col = 2 * LANES * j
        proj = jnp.dot(
            nrm[...], wv[a, :, col : col + 2 * LANES], preferred_element_type=jnp.float32
        )
        glu = (proj[:, :LANES] * jax.nn.sigmoid(proj[:, LANES:])).astype(jnp.bfloat16)
        g[PAD : PAD + frames, :] = glu.astype(jnp.float32)
        for r in range(0, frames, GROUP):
            mixed = jnp.zeros((GROUP, LANES), jnp.float32)
            for k in range(TAPS):
                mixed = mixed + g[r + k + 1 : r + k + 1 + GROUP, :] * kv[a, j, k : k + 1, :]
            kept = x[r : r + GROUP, :].astype(jnp.float32)
            y[r : r + GROUP, :] = (kept + mixed * jax.nn.sigmoid(mixed)).astype(jnp.bfloat16)

    def one_utt(i, carry):
        m = i // CORES
        ours = lax.rem(i, CORES) == core

        @pl.when((s == 0) & jnp.logical_not(ours))
        def _():
            init_in(m).wait_recv()

        @pl.when(s > 0)
        def _():
            for j in range(mine):
                hop(i, j).wait_recv()
                forward(i, j).start()
            for j in range(mine):
                forward_in(i, j).wait_recv()

        normalise(xin.at[i])

        for j in range(mine):
            at = core * mine + j
            chunk(0, xin.at[i, at], xmid.at[i, at], j)
            middle(i, j).start()

        @pl.when(i == 0)
        def _():
            gather_3(1)
            taps_of(1)

        for j in range(mine):
            middle_in(i, j).wait_recv()
        normalise(xmid.at[i])

        for j in range(mine):
            at = core * mine + j
            chunk(1, xmid.at[i, at], obuf.at[i, j], j)

            @pl.when(s < last)
            def _():
                hop(i, j).start()

            @pl.when((s == last) & jnp.logical_not(ours))
            def _():
                final(i, j).start()

        @pl.when((s == last) & ours)
        def _():
            ctx = jnp.zeros((frames, wctx_ref.shape[1]), jnp.float32)
            for j in range(mine):
                at = pl.ds(pl.multiple_of((core * mine + j) * LANES, LANES), LANES)
                ctx = ctx + jnp.dot(obuf[i, j], wctx_ref[at, :], preferred_element_type=jnp.float32)
            for j in range(mine):
                final(i, j).wait_recv()
                at = pl.ds(pl.multiple_of(((1 - core) * mine + j) * LANES, LANES), LANES)
                ctx = ctx + jnp.dot(pbuf[m, j], wctx_ref[at, :], preferred_element_type=jnp.float32)
            size = jnp.sum(ctx * ctx, axis=1, keepdims=True)
            cbuf[m] = (ctx * lax.rsqrt(size + 1e-06)).astype(jnp.bfloat16)
            for j in range(sections - 1):
                scatter(m, j).start()

        return carry

    lax.fori_loop(0, utts, one_utt, 0)

    def score(m, carry):
        @pl.when(s < last)
        def _():
            scatter(m, 0).wait_recv()

        @pl.when(s == last)
        def _():
            enc[m] = cbuf[m, last * share : (last + 1) * share, :]

        spots = lax.broadcasted_iota(jnp.int32, (share, frames), 1)
        rows_at = lax.broadcasted_iota(jnp.int32, (share, frames), 0) + s * share
        sims = 10.0 * lax.dot_general(
            enc[m], tgt[m], (((1,), (1,)), ((), ())), preferred_element_type=jnp.float32
        )
        positive = jnp.sum(jnp.where(spots == rows_at, sims, 0.0), axis=1, keepdims=True)
        negative = jnp.sum(cnt[m] * jnp.exp(sims), axis=1, keepdims=True)
        out_ref[m] = jnp.log(jnp.exp(positive) + negative) - positive
        return carry

    lax.fori_loop(0, micro, score, 0)

    for t in range(2):
        for h in range(CORES):

            @pl.when(jnp.logical_not(stays[t] & (core == h)))
            def _():
                own_out(t, h).wait_send()

    for a in range(2):
        for n in range(7):
            ring_out(a, n).wait_send()

    @pl.when(s == 0)
    def _():
        for m in range(micro):
            init(m).wait_send()

    def drain(i, carry):
        for j in range(mine):
            middle(i, j).wait_send()

            @pl.when(s < last)
            def _():
                hop(i, j).wait_send()

            @pl.when(s > 0)
            def _():
                forward(i, j).wait_send()

            @pl.when((s == last) & (lax.rem(i, CORES) != core))
            def _():
                final(i, j).wait_send()

        return carry

    lax.fori_loop(0, utts, drain, 0)

    @pl.when(s == last)
    def _():
        for m in range(micro):
            for j in range(sections - 1):
                scatter(m, j).wait_send()


def relay(sections, columns, feats, wcat, w_ctx, w_tgt, embed, starts, picks):
    micro, frames, width = feats.shape
    chunks = width // LANES
    share = frames // sections
    proj = w_ctx.shape[1]
    utts = CORES * micro
    mine = chunks // CORES
    half = width // CORES
    vmem = pl.BlockSpec(memory_space=pltpu.VMEM)
    smem = pl.BlockSpec(memory_space=pltpu.SMEM)
    dma = pltpu.SemaphoreType.DMA
    bf16 = jnp.bfloat16
    return pl.pallas_call(
        functools.partial(relay_kernel, sections, columns),
        out_shape=jax.ShapeDtypeStruct((micro, share, 1), jnp.float32),
        in_specs=[vmem, vmem, vmem, vmem, vmem, smem, vmem],
        out_specs=vmem,
        scratch_shapes=[
            pltpu.VMEM((utts, chunks, frames, LANES), bf16),
            pltpu.VMEM((utts, chunks, frames, LANES), bf16),
            pltpu.VMEM((utts, mine, frames, LANES), bf16),
            pltpu.VMEM((micro, mine, frames, LANES), bf16),
            pltpu.VMEM((frames, width), bf16),
            pltpu.VMEM((frames + 2 * PAD, LANES), jnp.float32),
            pltpu.VMEM((frames + 2 * PAD, LANES), jnp.float32),
            pltpu.VMEM((2, width, wcat.shape[3]), bf16),
            pltpu.VMEM((2, half // LANES, 32, LANES), jnp.float32),
            pltpu.VMEM((micro, frames, proj), bf16),
            pltpu.VMEM((micro, share, frames), jnp.float32),
            pltpu.VMEM((micro, share, proj), bf16),
            pltpu.VMEM((micro, frames, proj), bf16),
            dma((2, CORES)),
            dma((2, CORES)),
            dma((2, 7)),
            dma((2, 7)),
            dma((micro,)),
            dma((micro,)),
            dma((utts, mine)),
            dma((utts, mine)),
            dma((utts, mine)),
            dma((utts, mine)),
            dma((utts, mine)),
            dma((utts, mine)),
            dma((micro, mine)),
            dma((micro, mine)),
            dma((micro, sections)),
            dma((micro,)),
        ],
        compiler_params=pltpu.CompilerParams(
            collective_id=0, has_side_effects=True, vmem_limit_bytes=60 << 20
        ),
    )(feats, wcat, w_ctx, w_tgt, embed, starts, picks)


def on_device(feats, w_in, dw_kernel, mask_embed, w_ctx, w_tgt, mask_starts, distractors):
    sections = lax.axis_size("section")
    columns = lax.axis_size("fsdp")
    width = feats.shape[3]
    half = width // CORES

    taps = dw_kernel[:, 0].transpose(0, 2, 1)
    taps = jnp.pad(taps, ((0, 0), (0, 0), (0, LANES - taps.shape[2])))
    pairs = w_in[:, 0].reshape(2, -1, 2, CORES, half // LANES, LANES)
    pairs = pairs.transpose(0, 3, 1, 4, 2, 5).reshape(2, CORES, -1, 2 * half)
    taps = jnp.broadcast_to(taps[:, None], (2, CORES) + taps.shape[1:])
    wcat = jnp.concatenate([pairs, taps], axis=3)
    loss = relay(
        sections,
        columns,
        feats[:, 0],
        wcat,
        w_ctx,
        w_tgt,
        mask_embed[None, :],
        mask_starts[:, 0],
        distractors[:, 0],
    )
    return loss[:, :, 0][:, None, :]


def solution(mesh):
    placed = (
        P(None, "fsdp", None, None),
        P(None, "section", "fsdp", None),
        P(None, "section", None, "fsdp"),
        P(),
        P(),
        P(),
        P(None, "fsdp", None),
        P(None, "fsdp", "section", None),
    )
    return jax.shard_map(
        on_device, mesh=mesh, in_specs=placed, out_specs=P(None, "fsdp", "section"), check_vma=False
    )
```

```python
import functools

import jax
import jax.numpy as jnp
from jax import lax
from jax.experimental import pallas as pl
from jax.experimental.pallas import tpu as pltpu
from jax.sharding import PartitionSpec as P

MASK_LEN = 10
TAPS = 31
CW = 256
LANES = 128
PAD = 16
GROUP = 64
CORES = 2
MESH = pl.DeviceIdType.MESH


def relay_kernel(
    sections,
    columns,
    feats_hbm,
    wcat_ref,
    wctx_hbm,
    wtgt_hbm,
    embed_ref,
    starts_ref,
    picks_ref,
    out_ref,
    feats_ref,
    wctx_ref,
    wtgt_ref,
    load_sem,
    xin,
    xmid,
    obuf,
    pbuf,
    nrm,
    gbuf,
    wv,
    kv,
    tgt,
    cnt,
    enc,
    cbuf,
    own_send,
    own_recv,
    ring_send,
    ring_recv,
    init_send,
    init_recv,
    hop_send,
    hop_recv,
    fwd_send,
    fwd_recv,
    mid_send,
    mid_recv,
    fin_send,
    fin_recv,
    csend_sem,
    crecv_sem,
):
    utts, chunks, frames, _ = xin.shape
    micro = utts // CORES
    mine = chunks // CORES
    width = chunks * CW
    half = width // CORES
    share = frames // sections
    last = sections - 1
    rows = width // columns
    s = lax.axis_index("section")
    f = lax.axis_index("fsdp")
    core = lax.rem(f, 2)
    peer = f + 1 - 2 * core
    x_hi = lax.rem(f // 2, 2)
    across = f + 2 - 4 * x_hi
    y = f // 4
    ys = columns // 4
    up = lax.rem(f + 4, columns)
    down = lax.rem(f + columns - 4, columns)
    nxt = lax.rem(s + 1, sections)

    def load(src, dst, n):
        return pltpu.make_async_copy(src, dst, load_sem.at[n])

    load(feats_hbm, feats_ref, 0).start()
    load(wtgt_hbm, wtgt_ref, 1).start()
    load(wctx_hbm, wctx_ref, 2).start()

    barrier = pltpu.get_barrier_semaphore()
    for j in range(sections):

        @pl.when(s != j)
        def _():
            pl.semaphore_signal(
                barrier, inc=1, device_id={"section": j, "fsdp": f}, device_id_type=MESH
            )

        pl.semaphore_signal(
            barrier, inc=1, device_id={"section": j, "fsdp": peer}, device_id_type=MESH
        )
    for g in (up, down, across):
        pl.semaphore_signal(barrier, inc=1, device_id={"section": s, "fsdp": g}, device_id_type=MESH)
    pl.semaphore_wait(barrier, 2 * sections - 1 + 3)

    def remote(src, dst, send, recv, section, column):
        return pltpu.make_async_remote_copy(
            src_ref=src,
            dst_ref=dst,
            send_sem=send,
            recv_sem=recv,
            device_id={"section": section, "fsdp": column},
            device_id_type=MESH,
        )

    def rows_of(column):
        return pl.ds(pl.multiple_of(column * rows, 32), rows)

    def own_out(t, h):
        return remote(
            wcat_ref.at[t, h],
            wv.at[lax.rem(s, 2), rows_of(f)],
            own_send.at[t, h],
            own_recv.at[lax.rem(s, 2), core],
            s // 2 + (sections // 2) * t,
            f - core + h,
        )

    def own_here(t, h):
        return pltpu.make_async_copy(
            wcat_ref.at[t, h],
            wv.at[lax.rem(s, 2), rows_of(f)],
            own_recv.at[lax.rem(s, 2), core],
        )

    def own_in(a, c):
        return remote(
            wcat_ref.at[0, 0],
            wv.at[a, rows_of(f - core + c)],
            own_send.at[0, 0],
            own_recv.at[a, c],
            s,
            peer,
        )

    stays = [(s == 0), (s == last)]

    def send_own(t):
        for h in range(CORES):
            here = stays[t] & (core == h)

            @pl.when(here)
            def _():
                own_here(t, h).start()

            @pl.when(jnp.logical_not(here))
            def _():
                own_out(t, h).start()

    low = s < sections // 2
    send_own(0)

    @pl.when(jnp.logical_not(low))
    def _():
        send_own(1)

    def part(y_at, x_at, u):
        chip = lax.rem(y_at + 2 * ys, ys) * 2 + x_at
        return rows_of(CORES * chip + u)

    def ring(a, n, u, y_at, x_at, column):
        block = wv.at[a, part(y_at, x_at, u)]
        return remote(block, block, ring_send.at[a, n, u], ring_recv.at[a, n, u], s, column)

    other = 1 - x_hi

    def ring_out(a, n, u):
        y_at, x_at, column = (
            (y, x_hi, across),
            (y, x_hi, up),
            (y, x_hi, down),
            (y, other, up),
            (y, other, down),
            (y - 1, x_hi, up) if u == 0 else (y + 1, x_hi, down),
            (y + 2, x_hi, across),
        )[n]
        return ring(a, n, u, y_at, x_at, column)

    def ring_in(a, n, u):
        y_at, x_at, column = (
            (y, other, across),
            (y - 1, x_hi, up),
            (y + 1, x_hi, down),
            (y - 1, other, up),
            (y + 1, other, down),
            (y + 2, x_hi, up),
            (y + 2, other, across),
        )[n]
        return ring(a, n, u, y_at, x_at, column)

    def ring_start(a):
        for u in range(CORES):
            here = stays[a] & (core == u)

            @pl.when(here)
            def _():
                own_here(a, u).wait()

            @pl.when(jnp.logical_not(here))
            def _():
                own_in(a, u).wait_recv()

            for n in (0, 1, 2):
                ring_out(a, n, u).start()

    def pass_on(a, u, arrived, then):
        ring_in(a, arrived, u).wait_recv()
        for n in then:
            ring_out(a, n, u).start()

    def ring_pass(a):
        pass_on(a, 0, 1, (5,))
        pass_on(a, 1, 2, (5,))
        pass_on(a, 0, 0, (3, 4))
        pass_on(a, 1, 0, (3, 4))
        pass_on(a, 0, 5, (6,))
        pass_on(a, 1, 5, (6,))

    def ring_end(a):
        for u in range(CORES):
            for n in (2 - u, 3, 4, 6):
                ring_in(a, n, u).wait_recv()

    def init(m):
        at = xin.at[CORES * m + core]
        return remote(at, at, init_send.at[m], init_recv.at[m], s, peer)

    def init_in(m):
        at = xin.at[CORES * m + 1 - core]
        return remote(at, at, init_send.at[m], init_recv.at[m], s, peer)

    ring_start(0)

    def targets(m, carry):
        proj = jnp.dot(feats_ref[m], wtgt_ref[...], preferred_element_type=jnp.float32)
        size = jnp.sum(proj * proj, axis=1, keepdims=True)
        tgt[m] = (proj * lax.rsqrt(size + 1e-06)).astype(jnp.bfloat16)
        spots = lax.broadcasted_iota(jnp.int32, (share, frames), 1)
        total = jnp.zeros((share, frames), jnp.float32)
        for k in range(picks_ref.shape[2]):
            total = total + jnp.where(picks_ref[m, :, k : k + 1] == spots, 1.0, 0.0)
        cnt[m] = total
        return carry

    load(feats_hbm, feats_ref, 0).wait()
    load(wtgt_hbm, wtgt_ref, 1).wait()
    lax.fori_loop(0, micro, targets, 0)
    ring_pass(0)
    ring_start(1)

    @pl.when(low)
    def _():
        send_own(1)

    @pl.when(s == 0)
    def _():
        spot = lax.broadcasted_iota(jnp.int32, (frames, CW), 0)

        def one(m, carry):
            covered = jnp.zeros((frames, CW), jnp.int32)
            for j in range(starts_ref.shape[1]):
                start = starts_ref[m, j]
                inside = (spot >= start) & (spot < start + MASK_LEN)
                covered = jnp.where(inside, 1, covered)
            for c in range(chunks):
                embed = embed_ref[:, c * CW : (c + 1) * CW].astype(jnp.float32)
                seen = feats_ref[m, :, c * CW : (c + 1) * CW].astype(jnp.float32)
                xin[CORES * m + core, c] = jnp.where(covered > 0, embed, seen).astype(jnp.bfloat16)
            init(m).start()
            return carry

        lax.fori_loop(0, micro, one, 0)


    for b in range(CW // LANES):
        gbuf[b, 0:PAD, :] = jnp.zeros((PAD, LANES), jnp.float32)
        gbuf[b, PAD + frames : 2 * PAD + frames, :] = jnp.zeros((PAD, LANES), jnp.float32)

    ring_pass(1)
    load(wctx_hbm, wctx_ref, 2).wait()
    ring_end(0)

    def taps_of(a):
        for h in range(half // LANES):
            at = pl.ds(pl.multiple_of(core * half + h * LANES, LANES), LANES)
            block = wv[a, at, 2 * half : 2 * half + LANES]
            kv[a, h] = block.astype(jnp.float32).T[0:32, :]

    taps_of(0)

    def hop(i, j):
        return remote(
            obuf.at[i, j],
            xin.at[i, core * mine + j],
            hop_send.at[i, j],
            hop_recv.at[i, j],
            nxt,
            f,
        )

    def forward(i, j):
        at = xin.at[i, core * mine + j]
        return remote(at, at, fwd_send.at[i, j], fwd_recv.at[i, j], s, peer)

    def forward_in(i, j):
        at = xin.at[i, (1 - core) * mine + j]
        return remote(at, at, fwd_send.at[i, j], fwd_recv.at[i, j], s, peer)

    def middle(i, j):
        at = xmid.at[i, core * mine + j]
        return remote(at, at, mid_send.at[i, j], mid_recv.at[i, j], s, peer)

    def middle_in(i, j):
        at = xmid.at[i, (1 - core) * mine + j]
        return remote(at, at, mid_send.at[i, j], mid_recv.at[i, j], s, peer)

    def final(i, j):
        m = i // CORES
        return remote(obuf.at[i, j], pbuf.at[m, j], fin_send.at[m, j], fin_recv.at[m, j], s, peer)

    def scatter(m, j):
        return remote(
            cbuf.at[m, pl.ds(j * share, share)],
            enc.at[m],
            csend_sem.at[m, j],
            crecv_sem.at[m],
            j,
            f,
        )

    def normalise(x):
        total = jnp.zeros((frames, 1), jnp.float32)
        for c in range(chunks):
            total = total + jnp.sum(x[c].astype(jnp.float32), axis=1, keepdims=True)
        center = total / width
        total = jnp.zeros((frames, 1), jnp.float32)
        for c in range(chunks):
            off = x[c].astype(jnp.float32) - center
            total = total + jnp.sum(off * off, axis=1, keepdims=True)
        scale = lax.rsqrt(total / width + 1e-05)
        for c in range(chunks):
            off = x[c].astype(jnp.float32) - center
            nrm[:, c * CW : (c + 1) * CW] = (off * scale).astype(jnp.bfloat16)

    def chunk(a, x, y, j):
        col = pl.multiple_of(j * CW, CW)
        gate_col = pl.multiple_of(half + j * CW, CW)
        value = jnp.dot(nrm[...], wv[a, :, pl.ds(col, CW)], preferred_element_type=jnp.float32)
        gate = jnp.dot(nrm[...], wv[a, :, pl.ds(gate_col, CW)], preferred_element_type=jnp.float32)
        glu = (value * jax.nn.sigmoid(gate)).astype(jnp.bfloat16).astype(jnp.float32)
        for h in range(CW // LANES):
            gbuf[h, PAD : PAD + frames, :] = glu[:, h * LANES : (h + 1) * LANES]
        for h in range(CW // LANES):
            lane = slice(h * LANES, (h + 1) * LANES)
            for r in range(0, frames, GROUP):
                mixed = jnp.zeros((GROUP, LANES), jnp.float32)
                for k in range(TAPS):
                    taps = kv[a, j * (CW // LANES) + h, k : k + 1, :]
                    mixed = mixed + gbuf[h, r + k + 1 : r + k + 1 + GROUP, :] * taps
                kept = x[r : r + GROUP, lane].astype(jnp.float32)
                y[r : r + GROUP, lane] = (kept + mixed * jax.nn.sigmoid(mixed)).astype(jnp.bfloat16)

    def one_utt(i, carry):
        m = i // CORES
        ours = lax.rem(i, CORES) == core

        @pl.when((s == 0) & jnp.logical_not(ours))
        def _():
            init_in(m).wait_recv()

        @pl.when(s > 0)
        def _():
            for j in range(mine):
                hop(i, j).wait_recv()
                forward(i, j).start()
            for j in range(mine):
                forward_in(i, j).wait_recv()

        normalise(xin.at[i])

        def chunk_a(j, carry):
            at = core * mine + j
            chunk(0, xin.at[i, at], xmid.at[i, at], j)
            middle(i, j).start()
            return carry

        lax.fori_loop(0, mine, chunk_a, 0)

        @pl.when(i == 0)
        def _():
            ring_end(1)
            taps_of(1)

        for j in range(mine):
            middle_in(i, j).wait_recv()
        normalise(xmid.at[i])

        def chunk_b(j, carry):
            at = core * mine + j
            chunk(1, xmid.at[i, at], obuf.at[i, j], j)

            @pl.when(s < last)
            def _():
                hop(i, j).start()

            @pl.when((s == last) & jnp.logical_not(ours))
            def _():
                final(i, j).start()

            return carry

        lax.fori_loop(0, mine, chunk_b, 0)

        @pl.when((s == last) & ours)
        def _():
            ctx = jnp.zeros((frames, wctx_ref.shape[1]), jnp.float32)
            for j in range(mine):
                at = pl.ds(pl.multiple_of((core * mine + j) * CW, CW), CW)
                ctx = ctx + jnp.dot(obuf[i, j], wctx_ref[at, :], preferred_element_type=jnp.float32)
            for j in range(mine):
                final(i, j).wait_recv()
                at = pl.ds(pl.multiple_of(((1 - core) * mine + j) * CW, CW), CW)
                ctx = ctx + jnp.dot(pbuf[m, j], wctx_ref[at, :], preferred_element_type=jnp.float32)
            size = jnp.sum(ctx * ctx, axis=1, keepdims=True)
            cbuf[m] = (ctx * lax.rsqrt(size + 1e-06)).astype(jnp.bfloat16)
            for j in range(sections - 1):
                scatter(m, j).start()

        return carry

    lax.fori_loop(0, utts, one_utt, 0)

    def score(m, carry):
        @pl.when(s < last)
        def _():
            scatter(m, 0).wait_recv()

        @pl.when(s == last)
        def _():
            enc[m] = cbuf[m, last * share : (last + 1) * share, :]

        spots = lax.broadcasted_iota(jnp.int32, (share, frames), 1)
        rows_at = lax.broadcasted_iota(jnp.int32, (share, frames), 0) + s * share
        sims = 10.0 * lax.dot_general(
            enc[m], tgt[m], (((1,), (1,)), ((), ())), preferred_element_type=jnp.float32
        )
        positive = jnp.sum(jnp.where(spots == rows_at, sims, 0.0), axis=1, keepdims=True)
        negative = jnp.sum(cnt[m] * jnp.exp(sims), axis=1, keepdims=True)
        out_ref[m] = jnp.log(jnp.exp(positive) + negative) - positive
        return carry

    lax.fori_loop(0, micro, score, 0)

    for t in range(2):
        for h in range(CORES):

            @pl.when(jnp.logical_not(stays[t] & (core == h)))
            def _():
                own_out(t, h).wait_send()

    for a in range(2):
        for n in range(7):
            for u in range(CORES):
                ring_out(a, n, u).wait_send()

    @pl.when(s == 0)
    def _():
        for m in range(micro):
            init(m).wait_send()

    def drain(i, carry):
        for j in range(mine):
            middle(i, j).wait_send()

            @pl.when(s < last)
            def _():
                hop(i, j).wait_send()

            @pl.when(s > 0)
            def _():
                forward(i, j).wait_send()

            @pl.when((s == last) & (lax.rem(i, CORES) != core))
            def _():
                final(i, j).wait_send()

        return carry

    lax.fori_loop(0, utts, drain, 0)

    @pl.when(s == last)
    def _():
        for m in range(micro):
            for j in range(sections - 1):
                scatter(m, j).wait_send()


def relay(sections, columns, feats, wcat, w_ctx, w_tgt, embed, starts, picks):
    micro, frames, width = feats.shape
    chunks = width // CW
    share = frames // sections
    proj = w_ctx.shape[1]
    utts = CORES * micro
    mine = chunks // CORES
    half = width // CORES
    vmem = pl.BlockSpec(memory_space=pltpu.VMEM)
    smem = pl.BlockSpec(memory_space=pltpu.SMEM)
    hbm = pl.BlockSpec(memory_space=pl.ANY)
    dma = pltpu.SemaphoreType.DMA
    bf16 = jnp.bfloat16
    return pl.pallas_call(
        functools.partial(relay_kernel, sections, columns),
        out_shape=jax.ShapeDtypeStruct((micro, share, 1), jnp.float32),
        in_specs=[hbm, hbm, hbm, hbm, vmem, smem, vmem],
        out_specs=vmem,
        scratch_shapes=[
            pltpu.VMEM(feats.shape, bf16),
            pltpu.VMEM(w_ctx.shape, bf16),
            pltpu.VMEM(w_tgt.shape, bf16),
            dma((3,)),
            pltpu.VMEM((utts, chunks, frames, CW), bf16),
            pltpu.VMEM((utts, chunks, frames, CW), bf16),
            pltpu.VMEM((utts, mine, frames, CW), bf16),
            pltpu.VMEM((micro, mine, frames, CW), bf16),
            pltpu.VMEM((frames, width), bf16),
            pltpu.VMEM((CW // LANES, frames + 2 * PAD, LANES), jnp.float32),
            pltpu.VMEM((2, width, wcat.shape[3]), bf16),
            pltpu.VMEM((2, half // LANES, 32, LANES), jnp.float32),
            pltpu.VMEM((micro, frames, proj), bf16),
            pltpu.VMEM((micro, share, frames), jnp.float32),
            pltpu.VMEM((micro, share, proj), bf16),
            pltpu.VMEM((micro, frames, proj), bf16),
            dma((2, CORES)),
            dma((2, CORES)),
            dma((2, 7, CORES)),
            dma((2, 7, CORES)),
            dma((micro,)),
            dma((micro,)),
            dma((utts, mine)),
            dma((utts, mine)),
            dma((utts, mine)),
            dma((utts, mine)),
            dma((utts, mine)),
            dma((utts, mine)),
            dma((micro, mine)),
            dma((micro, mine)),
            dma((micro, sections)),
            dma((micro,)),
        ],
        compiler_params=pltpu.CompilerParams(
            collective_id=0, has_side_effects=True, vmem_limit_bytes=60 << 20
        ),
    )(feats, wcat, w_ctx, w_tgt, embed, starts, picks)


def on_device(feats, w_in, dw_kernel, mask_embed, w_ctx, w_tgt, mask_starts, distractors):
    sections = lax.axis_size("section")
    columns = lax.axis_size("fsdp")
    width = feats.shape[3]
    half = width // CORES

    taps = dw_kernel[:, 0].transpose(0, 2, 1)
    taps = jnp.pad(taps, ((0, 0), (0, 0), (0, LANES - taps.shape[2])))
    rows = w_in[:, 0]
    wcat = jnp.stack(
        [
            jnp.concatenate(
                [
                    rows[:, :, h * half : (h + 1) * half],
                    rows[:, :, width + h * half : width + (h + 1) * half],
                    taps,
                ],
                axis=2,
            )
            for h in range(CORES)
        ],
        axis=1,
    )
    loss = relay(
        sections,
        columns,
        feats[:, 0],
        wcat,
        w_ctx,
        w_tgt,
        mask_embed[None, :],
        mask_starts[:, 0],
        distractors[:, 0],
    )
    return loss[:, :, 0][:, None, :]


def solution(mesh):
    placed = (
        P(None, "fsdp", None, None),
        P(None, "section", "fsdp", None),
        P(None, "section", None, "fsdp"),
        P(),
        P(),
        P(),
        P(None, "fsdp", None),
        P(None, "fsdp", "section", None),
    )
    return jax.shard_map(
        on_device, mesh=mesh, in_specs=placed, out_specs=P(None, "fsdp", "section"), check_vma=False
    )
```

```python
import functools

import jax
import jax.numpy as jnp
from jax import lax
from jax.experimental import pallas as pl
from jax.experimental.pallas import tpu as pltpu
from jax.sharding import PartitionSpec as P

MASK_LEN = 10
TAPS = 31
CW = 256
LANES = 128
PAD = 16
GROUP = 64
CORES = 2
MESH = pl.DeviceIdType.MESH


def relay_kernel(
    sections,
    columns,
    feats_hbm,
    wcat_ref,
    wctx_hbm,
    wtgt_hbm,
    embed_ref,
    starts_ref,
    picks_ref,
    out_ref,
    feats_ref,
    wctx_ref,
    wtgt_ref,
    load_sem,
    xall,
    part_sum,
    gbuf,
    wsum,
    wv,
    kv,
    tgt,
    cnt,
    enc,
    cbuf,
    own_send,
    own_recv,
    ring_send,
    ring_recv,
    init_send,
    init_recv,
    hop_send,
    hop_recv,
    swap_send,
    swap_recv,
    csend_sem,
    crecv_sem,
):
    _, utts, _, frames, half = xall.shape
    micro = utts // CORES
    mine = half // CW
    width = half * CORES
    share = frames // sections
    last = sections - 1
    rows = width // columns
    s = lax.axis_index("section")
    f = lax.axis_index("fsdp")
    core = lax.rem(f, 2)
    peer = f + 1 - 2 * core
    x_hi = lax.rem(f // 2, 2)
    across = f + 2 - 4 * x_hi
    y = f // 4
    ys = columns // 4
    up = lax.rem(f + 4, columns)
    down = lax.rem(f + columns - 4, columns)
    nxt = lax.rem(s + 1, sections)

    def load(src, dst, n):
        return pltpu.make_async_copy(src, dst, load_sem.at[n])

    load(feats_hbm, feats_ref, 0).start()
    load(wtgt_hbm, wtgt_ref, 1).start()
    load(wctx_hbm, wctx_ref, 2).start()

    barrier = pltpu.get_barrier_semaphore()
    for j in range(sections):

        @pl.when(s != j)
        def _():
            pl.semaphore_signal(
                barrier, inc=1, device_id={"section": j, "fsdp": f}, device_id_type=MESH
            )

        pl.semaphore_signal(
            barrier, inc=1, device_id={"section": j, "fsdp": peer}, device_id_type=MESH
        )
    for g in (up, down, across):
        pl.semaphore_signal(barrier, inc=1, device_id={"section": s, "fsdp": g}, device_id_type=MESH)
    pl.semaphore_wait(barrier, 2 * sections - 1 + 3)

    def remote(src, dst, send, recv, section, column):
        return pltpu.make_async_remote_copy(
            src_ref=src,
            dst_ref=dst,
            send_sem=send,
            recv_sem=recv,
            device_id={"section": section, "fsdp": column},
            device_id_type=MESH,
        )

    def rows_of(column):
        return pl.ds(pl.multiple_of(column * rows, 32), rows)

    def own_out(t, h):
        return remote(
            wcat_ref.at[t, h],
            wv.at[lax.rem(s, 2), rows_of(f)],
            own_send.at[t, h],
            own_recv.at[lax.rem(s, 2), core],
            s // 2 + (sections // 2) * t,
            f - core + h,
        )

    def own_here(t, h):
        return pltpu.make_async_copy(
            wcat_ref.at[t, h],
            wv.at[lax.rem(s, 2), rows_of(f)],
            own_recv.at[lax.rem(s, 2), core],
        )

    def own_in(a, c):
        return remote(
            wcat_ref.at[0, 0],
            wv.at[a, rows_of(f - core + c)],
            own_send.at[0, 0],
            own_recv.at[a, c],
            s,
            peer,
        )

    stays = [(s == 0), (s == last)]

    def send_own(t):
        for h in range(CORES):
            here = stays[t] & (core == h)

            @pl.when(here)
            def _():
                own_here(t, h).start()

            @pl.when(jnp.logical_not(here))
            def _():
                own_out(t, h).start()

    send_own(0)
    send_own(1)

    def part(y_at, x_at, u):
        chip = lax.rem(y_at + 2 * ys, ys) * 2 + x_at
        return rows_of(CORES * chip + u)

    def ring(a, n, u, y_at, x_at, column):
        block = wv.at[a, part(y_at, x_at, u)]
        return remote(block, block, ring_send.at[a, n, u], ring_recv.at[a, n, u], s, column)

    other = 1 - x_hi

    def ring_out(a, n, u):
        y_at, x_at, column = (
            (y, x_hi, across),
            (y, x_hi, up),
            (y, x_hi, down),
            (y, other, up),
            (y, other, down),
            (y - 1, x_hi, up) if u == 0 else (y + 1, x_hi, down),
            (y + 2, x_hi, across),
        )[n]
        return ring(a, n, u, y_at, x_at, column)

    def ring_in(a, n, u):
        y_at, x_at, column = (
            (y, other, across),
            (y - 1, x_hi, up),
            (y + 1, x_hi, down),
            (y - 1, other, up),
            (y + 1, other, down),
            (y + 2, x_hi, up),
            (y + 2, other, across),
        )[n]
        return ring(a, n, u, y_at, x_at, column)

    def ring_start(a):
        for u in range(CORES):
            here = stays[a] & (core == u)

            @pl.when(here)
            def _():
                own_here(a, u).wait()

            @pl.when(jnp.logical_not(here))
            def _():
                own_in(a, u).wait_recv()

            for n in (0, 1, 2):
                ring_out(a, n, u).start()

    def pass_on(a, u, arrived, then):
        ring_in(a, arrived, u).wait_recv()
        for n in then:
            ring_out(a, n, u).start()

    def ring_pass(a):
        pass_on(a, 0, 1, (5,))
        pass_on(a, 1, 2, (5,))
        pass_on(a, 0, 0, (3, 4))
        pass_on(a, 1, 0, (3, 4))
        pass_on(a, 0, 5, (6,))
        pass_on(a, 1, 5, (6,))

    def ring_end(a):
        for u in range(CORES):
            for n in (2 - u, 3, 4, 6):
                ring_in(a, n, u).wait_recv()

    def init(m):
        at = xall.at[0, CORES * m + core]
        return remote(at, at, init_send.at[m], init_recv.at[m], s, peer)

    def init_in(m):
        at = xall.at[0, CORES * m + 1 - core]
        return remote(at, at, init_send.at[m], init_recv.at[m], s, peer)

    ring_start(0)

    def targets(m, carry):
        proj = jnp.dot(feats_ref[m], wtgt_ref[...], preferred_element_type=jnp.float32)
        size = jnp.sum(proj * proj, axis=1, keepdims=True)
        tgt[m] = (proj * lax.rsqrt(size + 1e-06)).astype(jnp.bfloat16)
        spots = lax.broadcasted_iota(jnp.int32, (share, frames), 1)
        total = jnp.zeros((share, frames), jnp.float32)
        for k in range(picks_ref.shape[2]):
            total = total + jnp.where(picks_ref[m, :, k : k + 1] == spots, 1.0, 0.0)
        cnt[m] = total
        return carry

    load(feats_hbm, feats_ref, 0).wait()
    load(wtgt_hbm, wtgt_ref, 1).wait()
    lax.fori_loop(0, micro, targets, 0)
    ring_pass(0)
    ring_start(1)

    @pl.when(s == 0)
    def _():
        spot = lax.broadcasted_iota(jnp.int32, (frames, CW), 0)

        def one(m, carry):
            covered = jnp.zeros((frames, CW), jnp.int32)
            for j in range(starts_ref.shape[1]):
                start = starts_ref[m, j]
                inside = (spot >= start) & (spot < start + MASK_LEN)
                covered = jnp.where(inside, 1, covered)
            for c in range(width // CW):
                embed = embed_ref[:, c * CW : (c + 1) * CW].astype(jnp.float32)
                seen = feats_ref[m, :, c * CW : (c + 1) * CW].astype(jnp.float32)
                at = slice(c % mine * CW, (c % mine + 1) * CW)
                xall[0, CORES * m + core, c // mine, :, at] = jnp.where(
                    covered > 0, embed, seen
                ).astype(jnp.bfloat16)
            init(m).start()
            return carry

        lax.fori_loop(0, micro, one, 0)


    for b in range(CW // LANES):
        gbuf[b, 0:PAD, :] = jnp.zeros((PAD, LANES), jnp.float32)
        gbuf[b, PAD + frames : 2 * PAD + frames, :] = jnp.zeros((PAD, LANES), jnp.float32)

    ring_pass(1)
    load(wctx_hbm, wctx_ref, 2).wait()
    ring_end(0)

    def prepare(a):
        for h in range(half // LANES):
            at = pl.ds(pl.multiple_of(core * half + h * LANES, LANES), LANES)
            block = wv[a, at, 2 * half : 2 * half + LANES]
            kv[a, h] = block.astype(jnp.float32).T[0:32, :]
        ones = jnp.ones((8, width), jnp.bfloat16)
        for c in range(2 * mine):
            at = slice(c * CW, (c + 1) * CW)
            wsum[a, :, at] = jnp.dot(ones, wv[a, :, at], preferred_element_type=jnp.float32)

    prepare(0)

    def piece(a, i, c, j):
        return xall.at[a, i, c, :, pl.ds(j * CW, CW)]

    def hop(i, j):
        return remote(
            piece(2, i, core, j),
            piece(0, i, core, j),
            hop_send.at[i, j],
            hop_recv.at[i, j],
            nxt,
            f,
        )

    def swap(a, i, j, c):
        at = piece(a, i, c, j)
        return remote(at, at, swap_send.at[a, i, j], swap_recv.at[a, i, j], s, peer)

    def swap_in(a, i):
        for j in range(mine):
            swap(a, i, j, 1 - core).wait_recv()

    def scatter(m, j):
        return remote(
            cbuf.at[m, pl.ds(j * share, share)],
            enc.at[m],
            csend_sem.at[m, j],
            crecv_sem.at[m],
            j,
            f,
        )

    def row_sum(v):
        return jnp.sum(v, axis=1, keepdims=True)

    def one_utt(i, carry):
        m = i // CORES
        ours = lax.rem(i, CORES) == core

        def layer(a, carry):
            @pl.when((s == 0) & (a == 0) & jnp.logical_not(ours))
            def _():
                init_in(m).wait_recv()

            @pl.when((s > 0) & (a == 0))
            def _():
                for j in range(mine):
                    hop(i, j).wait_recv()
                    swap(0, i, j, core).start()

            @pl.when((i == 0) & (a == 1))
            def _():
                ring_end(1)
                prepare(1)

            def product(c, col):
                at = pl.ds(pl.multiple_of(c * half, CW), half)
                return jnp.dot(
                    xall[a, i, c], wv[a, at, col], preferred_element_type=jnp.float32
                )

            def columns_of(j):
                value = pl.ds(j * CW, CW)
                gate = pl.ds(half + j * CW, CW)
                return value, gate

            def first(j, carry):
                value, gate = columns_of(j)
                part_sum[j, 0] = product(core, value)
                part_sum[j, 1] = product(core, gate)
                return carry

            for j in range(mine):
                first(j, 0)
            def block(c, j):
                return xall[a, i, c, :, j * CW : (j + 1) * CW].astype(jnp.float32)

            total = jnp.zeros((frames, 1), jnp.float32)
            for j in range(mine):
                total = total + row_sum(block(core, j))
            base = total / half
            square = jnp.zeros((frames, 1), jnp.float32)
            for j in range(mine):
                off = block(core, j) - base
                square = square + row_sum(off * off)

            @pl.when((s > 0) | (a > 0))
            def _():
                swap_in(a, i)

            moved = jnp.zeros((frames, CW), jnp.float32)
            far = jnp.zeros((frames, CW), jnp.float32)
            for j in range(mine):
                off = block(1 - core, j) - base
                moved = moved + off
                far = far + off * off
            shift = row_sum(moved) / width
            center = base + shift
            spread = (square + row_sum(far)) / width - shift * shift
            scale = lax.rsqrt(spread + 1e-05)

            def second(j, carry):
                value, gate = columns_of(j)
                v = part_sum[j, 0] + product(1 - core, value)
                v = (v - center * wsum[a, 0:1, value]) * scale
                g = part_sum[j, 1] + product(1 - core, gate)
                g = (g - center * wsum[a, 0:1, gate]) * scale
                glu = (v * jax.nn.sigmoid(g)).astype(jnp.bfloat16).astype(jnp.float32)
                for h in range(CW // LANES):
                    gbuf[h, PAD : PAD + frames, :] = glu[:, h * LANES : (h + 1) * LANES]
                for h in range(CW // LANES):
                    lane = pl.ds(j * CW + h * LANES, LANES)
                    for r in range(0, frames, GROUP):
                        mixed = jnp.zeros((GROUP, LANES), jnp.float32)
                        for k in range(TAPS):
                            taps = kv[a, j * (CW // LANES) + h, k : k + 1, :]
                            mixed = mixed + gbuf[h, r + k + 1 : r + k + 1 + GROUP, :] * taps
                        kept = xall[a, i, core, r : r + GROUP, lane].astype(jnp.float32)
                        xall[a + 1, i, core, r : r + GROUP, lane] = (
                            kept + mixed * jax.nn.sigmoid(mixed)
                        ).astype(jnp.bfloat16)

                @pl.when((a == 0) | ((s == last) & jnp.logical_not(ours)))
                def _():
                    swap(a + 1, i, j, core).start()

                @pl.when((a == 1) & (s < last))
                def _():
                    hop(i, j).start()

                return carry

            for j in range(mine):
                second(j, 0)
            return carry

        lax.fori_loop(0, 2, layer, 0)

        @pl.when((s == last) & ours)
        def _():
            def project(c):
                at = pl.ds(pl.multiple_of(c * half, CW), half)
                return jnp.dot(
                    xall[2, i, c], wctx_ref[at, :], preferred_element_type=jnp.float32
                )

            ctx = project(core)
            swap_in(2, i)
            ctx = ctx + project(1 - core)
            cbuf[m] = (ctx * lax.rsqrt(row_sum(ctx * ctx) + 1e-06)).astype(jnp.bfloat16)
            for j in range(sections - 1):
                scatter(m, j).start()

        return carry

    lax.fori_loop(0, utts, one_utt, 0)

    def score(m, carry):
        @pl.when(s < last)
        def _():
            scatter(m, 0).wait_recv()

        @pl.when(s == last)
        def _():
            enc[m] = cbuf[m, last * share : (last + 1) * share, :]

        spots = lax.broadcasted_iota(jnp.int32, (share, frames), 1)
        rows_at = lax.broadcasted_iota(jnp.int32, (share, frames), 0) + s * share
        sims = 10.0 * lax.dot_general(
            enc[m], tgt[m], (((1,), (1,)), ((), ())), preferred_element_type=jnp.float32
        )
        positive = jnp.sum(jnp.where(spots == rows_at, sims, 0.0), axis=1, keepdims=True)
        negative = jnp.sum(cnt[m] * jnp.exp(sims), axis=1, keepdims=True)
        out_ref[m] = jnp.log(jnp.exp(positive) + negative) - positive
        return carry

    lax.fori_loop(0, micro, score, 0)

    for t in range(2):
        for h in range(CORES):

            @pl.when(jnp.logical_not(stays[t] & (core == h)))
            def _():
                own_out(t, h).wait_send()

    for a in range(2):
        for n in range(7):
            for u in range(CORES):
                ring_out(a, n, u).wait_send()

    @pl.when(s == 0)
    def _():
        for m in range(micro):
            init(m).wait_send()

    def drain(i, carry):
        for j in range(mine):
            swap(1, i, j, core).wait_send()

            @pl.when(s < last)
            def _():
                hop(i, j).wait_send()

            @pl.when(s > 0)
            def _():
                swap(0, i, j, core).wait_send()

            @pl.when((s == last) & (lax.rem(i, CORES) != core))
            def _():
                swap(2, i, j, core).wait_send()

        return carry

    lax.fori_loop(0, utts, drain, 0)

    @pl.when(s == last)
    def _():
        for m in range(micro):
            for j in range(sections - 1):
                scatter(m, j).wait_send()


def relay(sections, columns, feats, wcat, w_ctx, w_tgt, embed, starts, picks):
    micro, frames, width = feats.shape
    share = frames // sections
    proj = w_ctx.shape[1]
    utts = CORES * micro
    half = width // CORES
    mine = half // CW
    vmem = pl.BlockSpec(memory_space=pltpu.VMEM)
    smem = pl.BlockSpec(memory_space=pltpu.SMEM)
    hbm = pl.BlockSpec(memory_space=pl.ANY)
    dma = pltpu.SemaphoreType.DMA
    bf16 = jnp.bfloat16
    return pl.pallas_call(
        functools.partial(relay_kernel, sections, columns),
        out_shape=jax.ShapeDtypeStruct((micro, share, 1), jnp.float32),
        in_specs=[hbm, hbm, hbm, hbm, vmem, smem, vmem],
        out_specs=vmem,
        scratch_shapes=[
            pltpu.VMEM(feats.shape, bf16),
            pltpu.VMEM(w_ctx.shape, bf16),
            pltpu.VMEM(w_tgt.shape, bf16),
            dma((3,)),
            pltpu.VMEM((3, utts, CORES, frames, half), bf16),
            pltpu.VMEM((mine, 2, frames, CW), jnp.float32),
            pltpu.VMEM((CW // LANES, frames + 2 * PAD, LANES), jnp.float32),
            pltpu.VMEM((2, 8, 2 * half), jnp.float32),
            pltpu.VMEM((2, width, wcat.shape[3]), bf16),
            pltpu.VMEM((2, half // LANES, 32, LANES), jnp.float32),
            pltpu.VMEM((micro, frames, proj), bf16),
            pltpu.VMEM((micro, share, frames), jnp.float32),
            pltpu.VMEM((micro, share, proj), bf16),
            pltpu.VMEM((micro, frames, proj), bf16),
            dma((2, CORES)),
            dma((2, CORES)),
            dma((2, 7, CORES)),
            dma((2, 7, CORES)),
            dma((micro,)),
            dma((micro,)),
            dma((utts, mine)),
            dma((utts, mine)),
            dma((3, utts, mine)),
            dma((3, utts, mine)),
            dma((micro, sections)),
            dma((micro,)),
        ],
        compiler_params=pltpu.CompilerParams(
            collective_id=0, has_side_effects=True, vmem_limit_bytes=60 << 20
        ),
    )(feats, wcat, w_ctx, w_tgt, embed, starts, picks)


def on_device(feats, w_in, dw_kernel, mask_embed, w_ctx, w_tgt, mask_starts, distractors):
    sections = lax.axis_size("section")
    columns = lax.axis_size("fsdp")
    width = feats.shape[3]
    half = width // CORES

    taps = dw_kernel[:, 0].transpose(0, 2, 1)
    taps = jnp.pad(taps, ((0, 0), (0, 0), (0, LANES - taps.shape[2])))
    rows = w_in[:, 0]
    wcat = jnp.stack(
        [
            jnp.concatenate(
                [
                    rows[:, :, h * half : (h + 1) * half],
                    rows[:, :, width + h * half : width + (h + 1) * half],
                    taps,
                ],
                axis=2,
            )
            for h in range(CORES)
        ],
        axis=1,
    )
    loss = relay(
        sections,
        columns,
        feats[:, 0],
        wcat,
        w_ctx,
        w_tgt,
        mask_embed[None, :],
        mask_starts[:, 0],
        distractors[:, 0],
    )
    return loss[:, :, 0][:, None, :]


def solution(mesh):
    placed = (
        P(None, "fsdp", None, None),
        P(None, "section", "fsdp", None),
        P(None, "section", None, "fsdp"),
        P(),
        P(),
        P(),
        P(None, "fsdp", None),
        P(None, "fsdp", "section", None),
    )
    return jax.shard_map(
        on_device, mesh=mesh, in_specs=placed, out_specs=P(None, "fsdp", "section"), check_vma=False
    )
```

```python
import functools

import jax
import jax.numpy as jnp
from jax import lax
from jax.experimental import pallas as pl
from jax.experimental.pallas import tpu as pltpu
from jax.sharding import PartitionSpec as P

MASK_LEN = 10
TAPS = 31
CW = 256
LANES = 128
PAD = 16
GROUP = 64
CORES = 2
MESH = pl.DeviceIdType.MESH


def relay_kernel(
    sections,
    columns,
    feats_hbm,
    wcat_ref,
    wctx_hbm,
    wtgt_hbm,
    embed_ref,
    starts_ref,
    picks_ref,
    out_ref,
    feats_ref,
    wctx_ref,
    wtgt_ref,
    load_sem,
    xall,
    part_sum,
    gbuf,
    wsum,
    wv,
    kv,
    tgt,
    cnt,
    enc,
    own_send,
    own_recv,
    ring_send,
    ring_recv,
    init_send,
    init_recv,
    hop_send,
    hop_recv,
    swap_send,
    swap_recv,
    csend_sem,
    crecv_sem,
):
    _, utts, _, frames, half = xall.shape
    micro = utts // CORES
    mine = half // CW
    width = half * CORES
    share = frames // sections
    last = sections - 1
    rows = width // columns
    s = lax.axis_index("section")
    f = lax.axis_index("fsdp")
    core = lax.rem(f, 2)
    peer = f + 1 - 2 * core
    x_hi = lax.rem(f // 2, 2)
    across = f + 2 - 4 * x_hi
    y = f // 4
    ys = columns // 4
    up = lax.rem(f + 4, columns)
    down = lax.rem(f + columns - 4, columns)
    nxt = lax.rem(s + 1, sections)

    def load(src, dst, n):
        return pltpu.make_async_copy(src, dst, load_sem.at[n])

    load(feats_hbm, feats_ref, 0).start()
    load(wtgt_hbm, wtgt_ref, 1).start()
    load(wctx_hbm, wctx_ref, 2).start()

    barrier = pltpu.get_barrier_semaphore()
    for j in range(sections):

        @pl.when(s != j)
        def _():
            pl.semaphore_signal(
                barrier, inc=1, device_id={"section": j, "fsdp": f}, device_id_type=MESH
            )

        pl.semaphore_signal(
            barrier, inc=1, device_id={"section": j, "fsdp": peer}, device_id_type=MESH
        )
    for g in (up, down, across):
        pl.semaphore_signal(barrier, inc=1, device_id={"section": s, "fsdp": g}, device_id_type=MESH)
    pl.semaphore_wait(barrier, 2 * sections - 1 + 3)

    def remote(src, dst, send, recv, section, column):
        return pltpu.make_async_remote_copy(
            src_ref=src,
            dst_ref=dst,
            send_sem=send,
            recv_sem=recv,
            device_id={"section": section, "fsdp": column},
            device_id_type=MESH,
        )

    def rows_of(column):
        return pl.ds(pl.multiple_of(column * rows, 32), rows)

    def own_out(t, h):
        return remote(
            wcat_ref.at[t, h],
            wv.at[lax.rem(s, 2), rows_of(f)],
            own_send.at[t, h],
            own_recv.at[lax.rem(s, 2), core],
            s // 2 + (sections // 2) * t,
            f - core + h,
        )

    def own_here(t, h):
        return pltpu.make_async_copy(
            wcat_ref.at[t, h],
            wv.at[lax.rem(s, 2), rows_of(f)],
            own_recv.at[lax.rem(s, 2), core],
        )

    def own_in(a, c):
        return remote(
            wcat_ref.at[0, 0],
            wv.at[a, rows_of(f - core + c)],
            own_send.at[0, 0],
            own_recv.at[a, c],
            s,
            peer,
        )

    stays = [(s == 0), (s == last)]

    def send_own(t):
        for h in range(CORES):
            here = stays[t] & (core == h)

            @pl.when(here)
            def _():
                own_here(t, h).start()

            @pl.when(jnp.logical_not(here))
            def _():
                own_out(t, h).start()

    send_own(0)
    send_own(1)

    def part(y_at, x_at, u):
        chip = lax.rem(y_at + 2 * ys, ys) * 2 + x_at
        return rows_of(CORES * chip + u)

    def ring(a, n, u, y_at, x_at, column):
        block = wv.at[a, part(y_at, x_at, u)]
        return remote(block, block, ring_send.at[a, n, u], ring_recv.at[a, n, u], s, column)

    other = 1 - x_hi

    def ring_out(a, n, u):
        y_at, x_at, column = (
            (y, x_hi, across),
            (y, x_hi, up),
            (y, x_hi, down),
            (y, other, up),
            (y, other, down),
            (y - 1, x_hi, up) if u == 0 else (y + 1, x_hi, down),
            (y + 2, x_hi, across),
        )[n]
        return ring(a, n, u, y_at, x_at, column)

    def ring_in(a, n, u):
        y_at, x_at, column = (
            (y, other, across),
            (y - 1, x_hi, up),
            (y + 1, x_hi, down),
            (y - 1, other, up),
            (y + 1, other, down),
            (y + 2, x_hi, up),
            (y + 2, other, across),
        )[n]
        return ring(a, n, u, y_at, x_at, column)

    def ring_start(a):
        for u in range(CORES):
            here = stays[a] & (core == u)

            @pl.when(here)
            def _():
                own_here(a, u).wait()

            @pl.when(jnp.logical_not(here))
            def _():
                own_in(a, u).wait_recv()

            for n in (0, 1, 2):
                ring_out(a, n, u).start()

    def pass_on(a, u, arrived, then):
        ring_in(a, arrived, u).wait_recv()
        for n in then:
            ring_out(a, n, u).start()

    def ring_pass(a):
        pass_on(a, 0, 1, (5,))
        pass_on(a, 1, 2, (5,))
        pass_on(a, 0, 0, (3, 4))
        pass_on(a, 1, 0, (3, 4))
        pass_on(a, 0, 5, (6,))
        pass_on(a, 1, 5, (6,))

    def ring_end(a):
        for u in range(CORES):
            for n in (2 - u, 3, 4, 6):
                ring_in(a, n, u).wait_recv()

    def init(m):
        at = xall.at[0, CORES * m + core]
        return remote(at, at, init_send.at[m], init_recv.at[m], s, peer)

    def init_in(m):
        at = xall.at[0, CORES * m + 1 - core]
        return remote(at, at, init_send.at[m], init_recv.at[m], s, peer)

    ring_start(0)

    def targets(m, carry):
        proj = jnp.dot(feats_ref[m], wtgt_ref[...], preferred_element_type=jnp.float32)
        size = jnp.sum(proj * proj, axis=1, keepdims=True)
        tgt[m] = (proj * lax.rsqrt(size + 1e-06)).astype(jnp.bfloat16)
        spots = lax.broadcasted_iota(jnp.int32, (share, frames), 1)
        total = jnp.zeros((share, frames), jnp.float32)
        for k in range(picks_ref.shape[2]):
            total = total + jnp.where(picks_ref[m, :, k : k + 1] == spots, 1.0, 0.0)
        cnt[m] = total
        return carry

    load(feats_hbm, feats_ref, 0).wait()
    load(wtgt_hbm, wtgt_ref, 1).wait()
    lax.fori_loop(0, micro, targets, 0)
    ring_pass(0)
    ring_start(1)

    @pl.when(s == 0)
    def _():
        spot = lax.broadcasted_iota(jnp.int32, (frames, CW), 0)

        def one(m, carry):
            covered = jnp.zeros((frames, CW), jnp.int32)
            for j in range(starts_ref.shape[1]):
                start = starts_ref[m, j]
                inside = (spot >= start) & (spot < start + MASK_LEN)
                covered = jnp.where(inside, 1, covered)
            for c in range(width // CW):
                embed = embed_ref[:, c * CW : (c + 1) * CW].astype(jnp.float32)
                seen = feats_ref[m, :, c * CW : (c + 1) * CW].astype(jnp.float32)
                at = slice(c % mine * CW, (c % mine + 1) * CW)
                xall[0, CORES * m + core, c // mine, :, at] = jnp.where(
                    covered > 0, embed, seen
                ).astype(jnp.bfloat16)
            init(m).start()
            return carry

        lax.fori_loop(0, micro, one, 0)


    for b in range(CW // LANES):
        gbuf[b, 0:PAD, :] = jnp.zeros((PAD, LANES), jnp.float32)
        gbuf[b, PAD + frames : 2 * PAD + frames, :] = jnp.zeros((PAD, LANES), jnp.float32)

    ring_pass(1)
    load(wctx_hbm, wctx_ref, 2).wait()
    ring_end(0)

    def prepare(a):
        for h in range(half // LANES):
            at = pl.ds(pl.multiple_of(core * half + h * LANES, LANES), LANES)
            block = wv[a, at, 2 * half : 2 * half + LANES]
            kv[a, h] = block.astype(jnp.float32).T[0:32, :]
        ones = jnp.ones((8, width), jnp.bfloat16)
        for c in range(2 * mine):
            at = slice(c * CW, (c + 1) * CW)
            wsum[a, :, at] = jnp.dot(ones, wv[a, :, at], preferred_element_type=jnp.float32)

    prepare(0)

    def piece(a, i, c, j):
        return xall.at[a, i, c, :, pl.ds(j * CW, CW)]

    def hop(i, j):
        return remote(
            piece(2, i, core, j),
            piece(0, i, core, j),
            hop_send.at[i, j],
            hop_recv.at[i, j],
            nxt,
            f,
        )

    def swap(a, i, j, c):
        at = piece(a, i, c, j)
        return remote(at, at, swap_send.at[a, i, j], swap_recv.at[a, i, j], s, peer)

    def swap_in(a, i):
        for j in range(mine):
            swap(a, i, j, 1 - core).wait_recv()

    def scatter(i, j):
        return remote(
            xall.at[2, i, core, pl.ds(j * share, share)],
            enc.at[i // CORES, core],
            csend_sem.at[i, j],
            crecv_sem.at[i // CORES, core],
            j,
            f - core + lax.rem(i, CORES),
        )

    def scatter_in(m, c):
        return remote(
            xall.at[2, 0, 0, pl.ds(0, share)],
            enc.at[m, c],
            csend_sem.at[0, 0],
            crecv_sem.at[m, c],
            s,
            peer,
        )

    def row_sum(v):
        return jnp.sum(v, axis=1, keepdims=True)

    def one_utt(i, carry):
        m = i // CORES
        ours = lax.rem(i, CORES) == core

        def layer(a, carry):
            @pl.when((s == 0) & (a == 0) & jnp.logical_not(ours))
            def _():
                init_in(m).wait_recv()

            @pl.when((s > 0) & (a == 0))
            def _():
                for j in range(mine):
                    hop(i, j).wait_recv()
                    swap(0, i, j, core).start()

            @pl.when((i == 0) & (a == 1))
            def _():
                ring_end(1)
                prepare(1)

            def product(c, col):
                at = pl.ds(pl.multiple_of(c * half, CW), half)
                return jnp.dot(
                    xall[a, i, c], wv[a, at, col], preferred_element_type=jnp.float32
                )

            def columns_of(j):
                value = pl.ds(j * CW, CW)
                gate = pl.ds(half + j * CW, CW)
                return value, gate

            def first(j, carry):
                value, gate = columns_of(j)
                part_sum[j, 0] = product(core, value)
                part_sum[j, 1] = product(core, gate)
                return carry

            for j in range(mine):
                first(j, 0)
            def block(c, j):
                return xall[a, i, c, :, j * CW : (j + 1) * CW].astype(jnp.float32)

            total = jnp.zeros((frames, 1), jnp.float32)
            for j in range(mine):
                total = total + row_sum(block(core, j))
            base = total / half
            square = jnp.zeros((frames, 1), jnp.float32)
            for j in range(mine):
                off = block(core, j) - base
                square = square + row_sum(off * off)

            @pl.when((s > 0) | (a > 0))
            def _():
                swap_in(a, i)

            moved = jnp.zeros((frames, CW), jnp.float32)
            far = jnp.zeros((frames, CW), jnp.float32)
            for j in range(mine):
                off = block(1 - core, j) - base
                moved = moved + off
                far = far + off * off
            shift = row_sum(moved) / width
            center = base + shift
            spread = (square + row_sum(far)) / width - shift * shift
            scale = lax.rsqrt(spread + 1e-05)

            def second(j, carry):
                value, gate = columns_of(j)
                v = part_sum[j, 0] + product(1 - core, value)
                v = (v - center * wsum[a, 0:1, value]) * scale
                g = part_sum[j, 1] + product(1 - core, gate)
                g = (g - center * wsum[a, 0:1, gate]) * scale
                glu = (v * jax.nn.sigmoid(g)).astype(jnp.bfloat16).astype(jnp.float32)
                for h in range(CW // LANES):
                    gbuf[h, PAD : PAD + frames, :] = glu[:, h * LANES : (h + 1) * LANES]
                for h in range(CW // LANES):
                    lane = pl.ds(j * CW + h * LANES, LANES)
                    for r in range(0, frames, GROUP):
                        mixed = jnp.zeros((GROUP, LANES), jnp.float32)
                        for k in range(TAPS):
                            taps = kv[a, j * (CW // LANES) + h, k : k + 1, :]
                            mixed = mixed + gbuf[h, r + k + 1 : r + k + 1 + GROUP, :] * taps
                        kept = xall[a, i, core, r : r + GROUP, lane].astype(jnp.float32)
                        xall[a + 1, i, core, r : r + GROUP, lane] = (
                            kept + mixed * jax.nn.sigmoid(mixed)
                        ).astype(jnp.bfloat16)

                @pl.when(a == 0)
                def _():
                    swap(1, i, j, core).start()

                @pl.when((a == 1) & (s < last))
                def _():
                    hop(i, j).start()

                return carry

            for j in range(mine):
                second(j, 0)
            return carry

        lax.fori_loop(0, 2, layer, 0)

        @pl.when(s == last)
        def _():
            for j in range(last):
                scatter(i, j).start()

            @pl.when(jnp.logical_not(ours))
            def _():
                scatter(i, last).start()

        return carry

    lax.fori_loop(0, utts, one_utt, 0)

    def score(m, carry):
        @pl.when(s < last)
        def _():
            scatter_in(m, core).wait_recv()

        @pl.when(s == last)
        def _():
            enc[m, core] = xall[2, CORES * m + core, core, last * share : (last + 1) * share, :]

        scatter_in(m, 1 - core).wait_recv()
        ctx = jnp.zeros((share, wctx_ref.shape[1]), jnp.float32)
        for c in range(CORES):
            ctx = ctx + jnp.dot(
                enc[m, c],
                wctx_ref[c * half : (c + 1) * half, :],
                preferred_element_type=jnp.float32,
            )
        ctx = (ctx * lax.rsqrt(row_sum(ctx * ctx) + 1e-06)).astype(jnp.bfloat16)
        spots = lax.broadcasted_iota(jnp.int32, (share, frames), 1)
        rows_at = lax.broadcasted_iota(jnp.int32, (share, frames), 0) + s * share
        sims = 10.0 * lax.dot_general(
            ctx, tgt[m], (((1,), (1,)), ((), ())), preferred_element_type=jnp.float32
        )
        positive = jnp.sum(jnp.where(spots == rows_at, sims, 0.0), axis=1, keepdims=True)
        negative = jnp.sum(cnt[m] * jnp.exp(sims), axis=1, keepdims=True)
        out_ref[m] = jnp.log(jnp.exp(positive) + negative) - positive
        return carry

    lax.fori_loop(0, micro, score, 0)

    for t in range(2):
        for h in range(CORES):

            @pl.when(jnp.logical_not(stays[t] & (core == h)))
            def _():
                own_out(t, h).wait_send()

    for a in range(2):
        for n in range(7):
            for u in range(CORES):
                ring_out(a, n, u).wait_send()

    @pl.when(s == 0)
    def _():
        for m in range(micro):
            init(m).wait_send()

    def drain(i, carry):
        for j in range(mine):
            swap(1, i, j, core).wait_send()

            @pl.when(s < last)
            def _():
                hop(i, j).wait_send()

            @pl.when(s > 0)
            def _():
                swap(0, i, j, core).wait_send()

        @pl.when(s == last)
        def _():
            for j in range(last):
                scatter(i, j).wait_send()

            @pl.when(lax.rem(i, CORES) != core)
            def _():
                scatter(i, last).wait_send()

        return carry

    lax.fori_loop(0, utts, drain, 0)


def relay(sections, columns, feats, wcat, w_ctx, w_tgt, embed, starts, picks):
    micro, frames, width = feats.shape
    share = frames // sections
    proj = w_ctx.shape[1]
    utts = CORES * micro
    half = width // CORES
    mine = half // CW
    vmem = pl.BlockSpec(memory_space=pltpu.VMEM)
    smem = pl.BlockSpec(memory_space=pltpu.SMEM)
    hbm = pl.BlockSpec(memory_space=pl.ANY)
    dma = pltpu.SemaphoreType.DMA
    bf16 = jnp.bfloat16
    return pl.pallas_call(
        functools.partial(relay_kernel, sections, columns),
        out_shape=jax.ShapeDtypeStruct((micro, share, 1), jnp.float32),
        in_specs=[hbm, hbm, hbm, hbm, vmem, smem, vmem],
        out_specs=vmem,
        scratch_shapes=[
            pltpu.VMEM(feats.shape, bf16),
            pltpu.VMEM(w_ctx.shape, bf16),
            pltpu.VMEM(w_tgt.shape, bf16),
            dma((3,)),
            pltpu.VMEM((3, utts, CORES, frames, half), bf16),
            pltpu.VMEM((mine, 2, frames, CW), jnp.float32),
            pltpu.VMEM((CW // LANES, frames + 2 * PAD, LANES), jnp.float32),
            pltpu.VMEM((2, 8, 2 * half), jnp.float32),
            pltpu.VMEM((2, width, wcat.shape[3]), bf16),
            pltpu.VMEM((2, half // LANES, 32, LANES), jnp.float32),
            pltpu.VMEM((micro, frames, proj), bf16),
            pltpu.VMEM((micro, share, frames), jnp.float32),
            pltpu.VMEM((micro, CORES, share, half), bf16),
            dma((2, CORES)),
            dma((2, CORES)),
            dma((2, 7, CORES)),
            dma((2, 7, CORES)),
            dma((micro,)),
            dma((micro,)),
            dma((utts, mine)),
            dma((utts, mine)),
            dma((2, utts, mine)),
            dma((2, utts, mine)),
            dma((utts, sections)),
            dma((micro, CORES)),
        ],
        compiler_params=pltpu.CompilerParams(
            collective_id=0, has_side_effects=True, vmem_limit_bytes=60 << 20
        ),
    )(feats, wcat, w_ctx, w_tgt, embed, starts, picks)


def on_device(feats, w_in, dw_kernel, mask_embed, w_ctx, w_tgt, mask_starts, distractors):
    sections = lax.axis_size("section")
    columns = lax.axis_size("fsdp")
    width = feats.shape[3]
    half = width // CORES

    taps = dw_kernel[:, 0].transpose(0, 2, 1)
    taps = jnp.pad(taps, ((0, 0), (0, 0), (0, LANES - taps.shape[2])))
    rows = w_in[:, 0]
    wcat = jnp.stack(
        [
            jnp.concatenate(
                [
                    rows[:, :, h * half : (h + 1) * half],
                    rows[:, :, width + h * half : width + (h + 1) * half],
                    taps,
                ],
                axis=2,
            )
            for h in range(CORES)
        ],
        axis=1,
    )
    loss = relay(
        sections,
        columns,
        feats[:, 0],
        wcat,
        w_ctx,
        w_tgt,
        mask_embed[None, :],
        mask_starts[:, 0],
        distractors[:, 0],
    )
    return loss[:, :, 0][:, None, :]


def solution(mesh):
    placed = (
        P(None, "fsdp", None, None),
        P(None, "section", "fsdp", None),
        P(None, "section", None, "fsdp"),
        P(),
        P(),
        P(),
        P(None, "fsdp", None),
        P(None, "fsdp", "section", None),
    )
    return jax.shard_map(
        on_device, mesh=mesh, in_specs=placed, out_specs=P(None, "fsdp", "section"), check_vma=False
    )
```

```python
import functools

import jax
import jax.numpy as jnp
from jax import lax
from jax.experimental import pallas as pl
from jax.experimental.pallas import tpu as pltpu
from jax.sharding import PartitionSpec as P

MASK_LEN = 10
TAPS = 31
CW = 256
LANES = 128
PAD = 16
GROUP = 64
CORES = 2
MESH = pl.DeviceIdType.MESH


def relay_kernel(
    sections,
    columns,
    feats_hbm,
    wcat_ref,
    wctx_hbm,
    wtgt_hbm,
    embed_ref,
    starts_ref,
    picks_ref,
    out_ref,
    feats_ref,
    wctx_ref,
    wtgt_ref,
    load_sem,
    xall,
    part_sum,
    gbuf,
    wsum,
    wv,
    kv,
    tgt,
    cnt,
    enc,
    own_send,
    own_recv,
    ring_send,
    ring_recv,
    init_send,
    init_recv,
    hop_send,
    hop_recv,
    swap_send,
    swap_recv,
    csend_sem,
    crecv_sem,
):
    _, utts, _, frames, half = xall.shape
    micro = utts // CORES
    mine = half // CW
    sent = half // LANES
    width = half * CORES
    share = frames // sections
    last = sections - 1
    rows = width // columns
    s = lax.axis_index("section")
    f = lax.axis_index("fsdp")
    core = lax.rem(f, 2)
    peer = f + 1 - 2 * core
    x_hi = lax.rem(f // 2, 2)
    across = f + 2 - 4 * x_hi
    y = f // 4
    ys = columns // 4
    up = lax.rem(f + 4, columns)
    down = lax.rem(f + columns - 4, columns)
    nxt = lax.rem(s + 1, sections)

    def load(src, dst, n):
        return pltpu.make_async_copy(src, dst, load_sem.at[n])

    load(feats_hbm, feats_ref, 0).start()
    load(wtgt_hbm, wtgt_ref, 1).start()
    load(wctx_hbm, wctx_ref, 2).start()

    barrier = pltpu.get_barrier_semaphore()
    for j in range(sections):

        @pl.when(s != j)
        def _():
            pl.semaphore_signal(
                barrier, inc=1, device_id={"section": j, "fsdp": f}, device_id_type=MESH
            )

        pl.semaphore_signal(
            barrier, inc=1, device_id={"section": j, "fsdp": peer}, device_id_type=MESH
        )
    for g in (up, down, across):
        pl.semaphore_signal(barrier, inc=1, device_id={"section": s, "fsdp": g}, device_id_type=MESH)
    pl.semaphore_wait(barrier, 2 * sections - 1 + 3)

    def remote(src, dst, send, recv, section, column):
        return pltpu.make_async_remote_copy(
            src_ref=src,
            dst_ref=dst,
            send_sem=send,
            recv_sem=recv,
            device_id={"section": section, "fsdp": column},
            device_id_type=MESH,
        )

    def rows_of(column):
        return pl.ds(pl.multiple_of(column * rows, 32), rows)

    def own_out(t, h):
        return remote(
            wcat_ref.at[t, h],
            wv.at[lax.rem(s, 2), rows_of(f)],
            own_send.at[t, h],
            own_recv.at[lax.rem(s, 2), core],
            s // 2 + (sections // 2) * t,
            f - core + h,
        )

    def own_here(t, h):
        return pltpu.make_async_copy(
            wcat_ref.at[t, h],
            wv.at[lax.rem(s, 2), rows_of(f)],
            own_recv.at[lax.rem(s, 2), core],
        )

    def own_in(a, c):
        return remote(
            wcat_ref.at[0, 0],
            wv.at[a, rows_of(f - core + c)],
            own_send.at[0, 0],
            own_recv.at[a, c],
            s,
            peer,
        )

    stays = [(s == 0), (s == last)]

    def send_own(t):
        for h in range(CORES):
            here = stays[t] & (core == h)

            @pl.when(here)
            def _():
                own_here(t, h).start()

            @pl.when(jnp.logical_not(here))
            def _():
                own_out(t, h).start()

    send_own(0)
    send_own(1)

    def part(y_at, x_at, u):
        chip = lax.rem(y_at + 2 * ys, ys) * 2 + x_at
        return rows_of(CORES * chip + u)

    def ring(a, n, u, y_at, x_at, column):
        block = wv.at[a, part(y_at, x_at, u)]
        return remote(block, block, ring_send.at[a, n, u], ring_recv.at[a, n, u], s, column)

    other = 1 - x_hi

    def ring_out(a, n, u):
        y_at, x_at, column = (
            (y, x_hi, across),
            (y, x_hi, up),
            (y, x_hi, down),
            (y, other, up),
            (y, other, down),
            (y - 1, x_hi, up) if u == 0 else (y + 1, x_hi, down),
            (y + 2, x_hi, across),
        )[n]
        return ring(a, n, u, y_at, x_at, column)

    def ring_in(a, n, u):
        y_at, x_at, column = (
            (y, other, across),
            (y - 1, x_hi, up),
            (y + 1, x_hi, down),
            (y - 1, other, up),
            (y + 1, other, down),
            (y + 2, x_hi, up),
            (y + 2, other, across),
        )[n]
        return ring(a, n, u, y_at, x_at, column)

    def ring_start(a):
        for u in range(CORES):
            here = stays[a] & (core == u)

            @pl.when(here)
            def _():
                own_here(a, u).wait()

            @pl.when(jnp.logical_not(here))
            def _():
                own_in(a, u).wait_recv()

            for n in (0, 1, 2):
                ring_out(a, n, u).start()

    def pass_on(a, u, arrived, then):
        ring_in(a, arrived, u).wait_recv()
        for n in then:
            ring_out(a, n, u).start()

    def ring_pass(a):
        pass_on(a, 0, 1, (5,))
        pass_on(a, 1, 2, (5,))
        pass_on(a, 0, 0, (3, 4))
        pass_on(a, 1, 0, (3, 4))
        pass_on(a, 0, 5, (6,))
        pass_on(a, 1, 5, (6,))

    def ring_end(a):
        for u in range(CORES):
            for n in (2 - u, 3, 4, 6):
                ring_in(a, n, u).wait_recv()

    def init(m):
        at = xall.at[0, CORES * m + core]
        return remote(at, at, init_send.at[m], init_recv.at[m], s, peer)

    def init_in(m):
        at = xall.at[0, CORES * m + 1 - core]
        return remote(at, at, init_send.at[m], init_recv.at[m], s, peer)

    ring_start(0)

    def targets(m, carry):
        proj = jnp.dot(feats_ref[m], wtgt_ref[...], preferred_element_type=jnp.float32)
        size = jnp.sum(proj * proj, axis=1, keepdims=True)
        tgt[m] = (proj * lax.rsqrt(size + 1e-06)).astype(jnp.bfloat16)
        spots = lax.broadcasted_iota(jnp.int32, (share, frames), 1)
        total = jnp.zeros((share, frames), jnp.float32)
        for k in range(picks_ref.shape[2]):
            total = total + jnp.where(picks_ref[m, :, k : k + 1] == spots, 1.0, 0.0)
        cnt[m] = total
        return carry

    load(feats_hbm, feats_ref, 0).wait()
    load(wtgt_hbm, wtgt_ref, 1).wait()
    lax.fori_loop(0, micro, targets, 0)
    ring_pass(0)
    ring_start(1)

    @pl.when(s == 0)
    def _():
        spot = lax.broadcasted_iota(jnp.int32, (frames, CW), 0)

        def one(m, carry):
            covered = jnp.zeros((frames, CW), jnp.int32)
            for j in range(starts_ref.shape[1]):
                start = starts_ref[m, j]
                inside = (spot >= start) & (spot < start + MASK_LEN)
                covered = jnp.where(inside, 1, covered)
            for c in range(width // CW):
                embed = embed_ref[:, c * CW : (c + 1) * CW].astype(jnp.float32)
                seen = feats_ref[m, :, c * CW : (c + 1) * CW].astype(jnp.float32)
                at = slice(c % mine * CW, (c % mine + 1) * CW)
                xall[0, CORES * m + core, c // mine, :, at] = jnp.where(
                    covered > 0, embed, seen
                ).astype(jnp.bfloat16)
            init(m).start()
            return carry

        lax.fori_loop(0, micro, one, 0)


    for b in range(CW // LANES):
        gbuf[b, 0:PAD, :] = jnp.zeros((PAD, LANES), jnp.float32)
        gbuf[b, PAD + frames : 2 * PAD + frames, :] = jnp.zeros((PAD, LANES), jnp.float32)

    ring_pass(1)
    load(wctx_hbm, wctx_ref, 2).wait()
    ring_end(0)

    def prepare(a):
        for h in range(half // LANES):
            at = pl.ds(pl.multiple_of(core * half + h * LANES, LANES), LANES)
            block = wv[a, at, 2 * half : 2 * half + LANES]
            kv[a, h] = block.astype(jnp.float32).T[0:32, :]
        ones = jnp.ones((8, width), jnp.bfloat16)
        for c in range(2 * mine):
            at = slice(c * CW, (c + 1) * CW)
            wsum[a, :, at] = jnp.dot(ones, wv[a, :, at], preferred_element_type=jnp.float32)

    prepare(0)

    def piece(a, i, c, j):
        return xall.at[a, i, c, :, pl.ds(j * LANES, LANES)]

    def hop(i, j):
        return remote(
            piece(2, i, core, j),
            piece(0, i, core, j),
            hop_send.at[i, j],
            hop_recv.at[i, j],
            nxt,
            f,
        )

    def swap(a, i, j, c):
        at = piece(a, i, c, j)
        return remote(at, at, swap_send.at[a, i, j], swap_recv.at[a, i, j], s, peer)

    def swap_in(a, i):
        for j in range(sent):
            swap(a, i, j, 1 - core).wait_recv()

    def scatter(i, j):
        return remote(
            xall.at[2, i, core, pl.ds(j * share, share)],
            enc.at[i // CORES, core],
            csend_sem.at[i, j],
            crecv_sem.at[i // CORES, core],
            j,
            f - core + lax.rem(i, CORES),
        )

    def scatter_in(m, c):
        return remote(
            xall.at[2, 0, 0, pl.ds(0, share)],
            enc.at[m, c],
            csend_sem.at[0, 0],
            crecv_sem.at[m, c],
            s,
            peer,
        )

    def row_sum(v):
        return jnp.sum(v, axis=1, keepdims=True)

    def one_utt(i, carry):
        m = i // CORES
        ours = lax.rem(i, CORES) == core

        def layer(a, carry):
            @pl.when((s == 0) & (a == 0) & jnp.logical_not(ours))
            def _():
                init_in(m).wait_recv()

            @pl.when((s > 0) & (a == 0))
            def _():
                for j in range(sent):
                    hop(i, j).wait_recv()
                    swap(0, i, j, core).start()

            @pl.when((i == 0) & (a == 1))
            def _():
                ring_end(1)
                prepare(1)

            def product(c, col):
                at = pl.ds(pl.multiple_of(c * half, CW), half)
                return jnp.dot(
                    xall[a, i, c], wv[a, at, col], preferred_element_type=jnp.float32
                )

            def columns_of(j):
                value = pl.ds(j * CW, CW)
                gate = pl.ds(half + j * CW, CW)
                return value, gate

            def first(j, carry):
                value, gate = columns_of(j)
                part_sum[j, 0] = product(core, value)
                part_sum[j, 1] = product(core, gate)
                return carry

            for j in range(mine):
                first(j, 0)
            def block(c, j):
                return xall[a, i, c, :, j * CW : (j + 1) * CW].astype(jnp.float32)

            total = jnp.zeros((frames, 1), jnp.float32)
            for j in range(mine):
                total = total + row_sum(block(core, j))
            base = total / half
            square = jnp.zeros((frames, 1), jnp.float32)
            for j in range(mine):
                off = block(core, j) - base
                square = square + row_sum(off * off)

            @pl.when((s > 0) | (a > 0))
            def _():
                swap_in(a, i)

            moved = jnp.zeros((frames, CW), jnp.float32)
            far = jnp.zeros((frames, CW), jnp.float32)
            for j in range(mine):
                off = block(1 - core, j) - base
                moved = moved + off
                far = far + off * off
            shift = row_sum(moved) / width
            center = base + shift
            spread = (square + row_sum(far)) / width - shift * shift
            scale = lax.rsqrt(spread + 1e-05)

            def second(j, carry):
                value, gate = columns_of(j)
                v = part_sum[j, 0] + product(1 - core, value)
                v = (v - center * wsum[a, 0:1, value]) * scale
                g = part_sum[j, 1] + product(1 - core, gate)
                g = (g - center * wsum[a, 0:1, gate]) * scale
                glu = (v * jax.nn.sigmoid(g)).astype(jnp.bfloat16).astype(jnp.float32)
                for h in range(CW // LANES):
                    gbuf[h, PAD : PAD + frames, :] = glu[:, h * LANES : (h + 1) * LANES]
                for h in range(CW // LANES):
                    lane = pl.ds(j * CW + h * LANES, LANES)
                    for r in range(0, frames, GROUP):
                        mixed = jnp.zeros((GROUP, LANES), jnp.float32)
                        for k in range(TAPS):
                            taps = kv[a, j * (CW // LANES) + h, k : k + 1, :]
                            mixed = mixed + gbuf[h, r + k + 1 : r + k + 1 + GROUP, :] * taps
                        kept = xall[a, i, core, r : r + GROUP, lane].astype(jnp.float32)
                        xall[a + 1, i, core, r : r + GROUP, lane] = (
                            kept + mixed * jax.nn.sigmoid(mixed)
                        ).astype(jnp.bfloat16)

                    @pl.when(a == 0)
                    def _():
                        swap(1, i, j * (CW // LANES) + h, core).start()

                    @pl.when((a == 1) & (s < last))
                    def _():
                        hop(i, j * (CW // LANES) + h).start()

                return carry

            for j in range(mine):
                second(j, 0)
            return carry

        lax.fori_loop(0, 2, layer, 0)

        @pl.when(s == last)
        def _():
            for j in range(last):
                scatter(i, j).start()

            @pl.when(jnp.logical_not(ours))
            def _():
                scatter(i, last).start()

        return carry

    lax.fori_loop(0, utts, one_utt, 0)

    def score(m, carry):
        @pl.when(s < last)
        def _():
            scatter_in(m, core).wait_recv()

        @pl.when(s == last)
        def _():
            enc[m, core] = xall[2, CORES * m + core, core, last * share : (last + 1) * share, :]

        scatter_in(m, 1 - core).wait_recv()
        ctx = jnp.zeros((share, wctx_ref.shape[1]), jnp.float32)
        for c in range(CORES):
            ctx = ctx + jnp.dot(
                enc[m, c],
                wctx_ref[c * half : (c + 1) * half, :],
                preferred_element_type=jnp.float32,
            )
        ctx = (ctx * lax.rsqrt(row_sum(ctx * ctx) + 1e-06)).astype(jnp.bfloat16)
        spots = lax.broadcasted_iota(jnp.int32, (share, frames), 1)
        rows_at = lax.broadcasted_iota(jnp.int32, (share, frames), 0) + s * share
        sims = 10.0 * lax.dot_general(
            ctx, tgt[m], (((1,), (1,)), ((), ())), preferred_element_type=jnp.float32
        )
        positive = jnp.sum(jnp.where(spots == rows_at, sims, 0.0), axis=1, keepdims=True)
        negative = jnp.sum(cnt[m] * jnp.exp(sims), axis=1, keepdims=True)
        out_ref[m] = jnp.log(jnp.exp(positive) + negative) - positive
        return carry

    lax.fori_loop(0, micro, score, 0)

    for t in range(2):
        for h in range(CORES):

            @pl.when(jnp.logical_not(stays[t] & (core == h)))
            def _():
                own_out(t, h).wait_send()

    for a in range(2):
        for n in range(7):
            for u in range(CORES):
                ring_out(a, n, u).wait_send()

    @pl.when(s == 0)
    def _():
        for m in range(micro):
            init(m).wait_send()

    def drain(i, carry):
        for j in range(sent):
            swap(1, i, j, core).wait_send()

            @pl.when(s < last)
            def _():
                hop(i, j).wait_send()

            @pl.when(s > 0)
            def _():
                swap(0, i, j, core).wait_send()

        @pl.when(s == last)
        def _():
            for j in range(last):
                scatter(i, j).wait_send()

            @pl.when(lax.rem(i, CORES) != core)
            def _():
                scatter(i, last).wait_send()

        return carry

    lax.fori_loop(0, utts, drain, 0)


def relay(sections, columns, feats, wcat, w_ctx, w_tgt, embed, starts, picks):
    micro, frames, width = feats.shape
    share = frames // sections
    proj = w_ctx.shape[1]
    utts = CORES * micro
    half = width // CORES
    mine = half // CW
    vmem = pl.BlockSpec(memory_space=pltpu.VMEM)
    smem = pl.BlockSpec(memory_space=pltpu.SMEM)
    hbm = pl.BlockSpec(memory_space=pl.ANY)
    dma = pltpu.SemaphoreType.DMA
    bf16 = jnp.bfloat16
    return pl.pallas_call(
        functools.partial(relay_kernel, sections, columns),
        out_shape=jax.ShapeDtypeStruct((micro, share, 1), jnp.float32),
        in_specs=[hbm, hbm, hbm, hbm, vmem, smem, vmem],
        out_specs=vmem,
        scratch_shapes=[
            pltpu.VMEM(feats.shape, bf16),
            pltpu.VMEM(w_ctx.shape, bf16),
            pltpu.VMEM(w_tgt.shape, bf16),
            dma((3,)),
            pltpu.VMEM((3, utts, CORES, frames, half), bf16),
            pltpu.VMEM((mine, 2, frames, CW), jnp.float32),
            pltpu.VMEM((CW // LANES, frames + 2 * PAD, LANES), jnp.float32),
            pltpu.VMEM((2, 8, 2 * half), jnp.float32),
            pltpu.VMEM((2, width, wcat.shape[3]), bf16),
            pltpu.VMEM((2, half // LANES, 32, LANES), jnp.float32),
            pltpu.VMEM((micro, frames, proj), bf16),
            pltpu.VMEM((micro, share, frames), jnp.float32),
            pltpu.VMEM((micro, CORES, share, half), bf16),
            dma((2, CORES)),
            dma((2, CORES)),
            dma((2, 7, CORES)),
            dma((2, 7, CORES)),
            dma((micro,)),
            dma((micro,)),
            dma((utts, half // LANES)),
            dma((utts, half // LANES)),
            dma((2, utts, half // LANES)),
            dma((2, utts, half // LANES)),
            dma((utts, sections)),
            dma((micro, CORES)),
        ],
        compiler_params=pltpu.CompilerParams(
            collective_id=0, has_side_effects=True, vmem_limit_bytes=60 << 20
        ),
    )(feats, wcat, w_ctx, w_tgt, embed, starts, picks)


def on_device(feats, w_in, dw_kernel, mask_embed, w_ctx, w_tgt, mask_starts, distractors):
    sections = lax.axis_size("section")
    columns = lax.axis_size("fsdp")
    width = feats.shape[3]
    half = width // CORES

    taps = dw_kernel[:, 0].transpose(0, 2, 1)
    taps = jnp.pad(taps, ((0, 0), (0, 0), (0, LANES - taps.shape[2])))
    rows = w_in[:, 0]
    wcat = jnp.stack(
        [
            jnp.concatenate(
                [
                    rows[:, :, h * half : (h + 1) * half],
                    rows[:, :, width + h * half : width + (h + 1) * half],
                    taps,
                ],
                axis=2,
            )
            for h in range(CORES)
        ],
        axis=1,
    )
    loss = relay(
        sections,
        columns,
        feats[:, 0],
        wcat,
        w_ctx,
        w_tgt,
        mask_embed[None, :],
        mask_starts[:, 0],
        distractors[:, 0],
    )
    return loss[:, :, 0][:, None, :]


def solution(mesh):
    placed = (
        P(None, "fsdp", None, None),
        P(None, "section", "fsdp", None),
        P(None, "section", None, "fsdp"),
        P(),
        P(),
        P(),
        P(None, "fsdp", None),
        P(None, "fsdp", "section", None),
    )
    return jax.shard_map(
        on_device, mesh=mesh, in_specs=placed, out_specs=P(None, "fsdp", "section"), check_vma=False
    )
```

```python
import functools

import jax
import jax.numpy as jnp
from jax import lax
from jax.experimental import pallas as pl
from jax.experimental.pallas import tpu as pltpu
from jax.sharding import PartitionSpec as P

MASK_LEN = 10
TAPS = 31
CW = 256
LANES = 128
PAD = 16
GROUP = 64
CORES = 2
MESH = pl.DeviceIdType.MESH


def relay_kernel(
    sections,
    columns,
    feats_hbm,
    w_hbm,
    taps_hbm,
    wctx_hbm,
    wtgt_hbm,
    embed_ref,
    starts_ref,
    picks_ref,
    out_ref,
    feats_ref,
    wctx_ref,
    wtgt_ref,
    load_sem,
    xall,
    part_sum,
    gbuf,
    wsum,
    wv,
    kv,
    tgt,
    cnt,
    enc,
    own_send,
    own_recv,
    ring_send,
    ring_recv,
    init_send,
    init_recv,
    hop_send,
    hop_recv,
    swap_send,
    swap_recv,
    csend_sem,
    crecv_sem,
):
    _, utts, _, frames, half = xall.shape
    micro = utts // CORES
    mine = half // CW
    sent = half // LANES
    width = half * CORES
    share = frames // sections
    last = sections - 1
    rows = width // columns
    s = lax.axis_index("section")
    f = lax.axis_index("fsdp")
    core = lax.rem(f, 2)
    peer = f + 1 - 2 * core
    x_hi = lax.rem(f // 2, 2)
    across = f + 2 - 4 * x_hi
    y = f // 4
    ys = columns // 4
    up = lax.rem(f + 4, columns)
    down = lax.rem(f + columns - 4, columns)
    nxt = lax.rem(s + 1, sections)

    def load(src, dst, n):
        return pltpu.make_async_copy(src, dst, load_sem.at[n])

    load(feats_hbm, feats_ref, 0).start()
    load(wtgt_hbm, wtgt_ref, 1).start()
    load(wctx_hbm, wctx_ref, 2).start()

    barrier = pltpu.get_barrier_semaphore()
    for j in range(sections):

        @pl.when(s != j)
        def _():
            pl.semaphore_signal(
                barrier, inc=1, device_id={"section": j, "fsdp": f}, device_id_type=MESH
            )

        pl.semaphore_signal(
            barrier, inc=1, device_id={"section": j, "fsdp": peer}, device_id_type=MESH
        )
    for g in (up, down, across):
        pl.semaphore_signal(barrier, inc=1, device_id={"section": s, "fsdp": g}, device_id_type=MESH)
    pl.semaphore_wait(barrier, 2 * sections - 1 + 3)

    def remote(src, dst, send, recv, section, column):
        return pltpu.make_async_remote_copy(
            src_ref=src,
            dst_ref=dst,
            send_sem=send,
            recv_sem=recv,
            device_id={"section": section, "fsdp": column},
            device_id_type=MESH,
        )

    def rows_of(column):
        return pl.ds(pl.multiple_of(column * rows, 32), rows)

    def own_parts(t, h, a, at):
        low_half, high_half = slice(0, half), slice(half, 2 * half)
        return (
            (w_hbm.at[t, :, h * half : (h + 1) * half], wv.at[a, at, low_half]),
            (w_hbm.at[t, :, width + h * half : width + (h + 1) * half], wv.at[a, at, high_half]),
            (taps_hbm.at[t], wv.at[a, at, 2 * half : 2 * half + LANES]),
        )

    def own_out(t, h, p):
        src, dst = own_parts(t, h, lax.rem(s, 2), rows_of(f))[p]
        return remote(
            src,
            dst,
            own_send.at[t, h, p],
            own_recv.at[lax.rem(s, 2), core, p],
            s // 2 + (sections // 2) * t,
            f - core + h,
        )

    def own_here(t, h, p):
        src, dst = own_parts(t, h, lax.rem(s, 2), rows_of(f))[p]
        return pltpu.make_async_copy(src, dst, own_recv.at[lax.rem(s, 2), core, p])

    def own_in(a, c, p):
        src, dst = own_parts(0, 0, a, rows_of(f - core + c))[p]
        return remote(src, dst, own_send.at[0, 0, p], own_recv.at[a, c, p], s, peer)

    stays = [(s == 0), (s == last)]

    def send_own(t):
        for h in range(CORES):
            here = stays[t] & (core == h)

            @pl.when(here)
            def _():
                for p in range(3):
                    own_here(t, h, p).start()

            @pl.when(jnp.logical_not(here))
            def _():
                for p in range(3):
                    own_out(t, h, p).start()

    send_own(0)
    send_own(1)

    def part(y_at, x_at, u):
        chip = lax.rem(y_at + 2 * ys, ys) * 2 + x_at
        return rows_of(CORES * chip + u)

    def ring(a, n, u, y_at, x_at, column):
        block = wv.at[a, part(y_at, x_at, u)]
        return remote(block, block, ring_send.at[a, n, u], ring_recv.at[a, n, u], s, column)

    other = 1 - x_hi

    def ring_out(a, n, u):
        y_at, x_at, column = (
            (y, x_hi, across),
            (y, x_hi, up),
            (y, x_hi, down),
            (y, other, up),
            (y, other, down),
            (y - 1, x_hi, up) if u == 0 else (y + 1, x_hi, down),
            (y + 2, x_hi, across),
        )[n]
        return ring(a, n, u, y_at, x_at, column)

    def ring_in(a, n, u):
        y_at, x_at, column = (
            (y, other, across),
            (y - 1, x_hi, up),
            (y + 1, x_hi, down),
            (y - 1, other, up),
            (y + 1, other, down),
            (y + 2, x_hi, up),
            (y + 2, other, across),
        )[n]
        return ring(a, n, u, y_at, x_at, column)

    def ring_start(a):
        for u in range(CORES):
            here = stays[a] & (core == u)

            @pl.when(here)
            def _():
                for p in range(3):
                    own_here(a, u, p).wait()

            @pl.when(jnp.logical_not(here))
            def _():
                for p in range(3):
                    own_in(a, u, p).wait_recv()

            for n in (0, 1, 2):
                ring_out(a, n, u).start()

    def pass_on(a, u, arrived, then):
        ring_in(a, arrived, u).wait_recv()
        for n in then:
            ring_out(a, n, u).start()

    def ring_pass(a):
        pass_on(a, 0, 1, (5,))
        pass_on(a, 1, 2, (5,))
        pass_on(a, 0, 0, (3, 4))
        pass_on(a, 1, 0, (3, 4))
        pass_on(a, 0, 5, (6,))
        pass_on(a, 1, 5, (6,))

    def ring_end(a):
        for u in range(CORES):
            for n in (2 - u, 3, 4, 6):
                ring_in(a, n, u).wait_recv()

    def init(m):
        at = xall.at[0, CORES * m + core]
        return remote(at, at, init_send.at[m], init_recv.at[m], s, peer)

    def init_in(m):
        at = xall.at[0, CORES * m + 1 - core]
        return remote(at, at, init_send.at[m], init_recv.at[m], s, peer)

    ring_start(0)

    def targets(m, carry):
        proj = jnp.dot(feats_ref[m], wtgt_ref[...], preferred_element_type=jnp.float32)
        size = jnp.sum(proj * proj, axis=1, keepdims=True)
        tgt[m] = (proj * lax.rsqrt(size + 1e-06)).astype(jnp.bfloat16)
        spots = lax.broadcasted_iota(jnp.int32, (share, frames), 1)
        total = jnp.zeros((share, frames), jnp.float32)
        for k in range(picks_ref.shape[2]):
            total = total + jnp.where(picks_ref[m, :, k : k + 1] == spots, 1.0, 0.0)
        cnt[m] = total
        return carry

    load(feats_hbm, feats_ref, 0).wait()
    load(wtgt_hbm, wtgt_ref, 1).wait()
    lax.fori_loop(0, micro, targets, 0)
    ring_pass(0)
    ring_start(1)

    @pl.when(s == 0)
    def _():
        spot = lax.broadcasted_iota(jnp.int32, (frames, CW), 0)

        def one(m, carry):
            covered = jnp.zeros((frames, CW), jnp.int32)
            for j in range(starts_ref.shape[1]):
                start = starts_ref[m, j]
                inside = (spot >= start) & (spot < start + MASK_LEN)
                covered = jnp.where(inside, 1, covered)
            for c in range(width // CW):
                embed = embed_ref[:, c * CW : (c + 1) * CW].astype(jnp.float32)
                seen = feats_ref[m, :, c * CW : (c + 1) * CW].astype(jnp.float32)
                at = slice(c % mine * CW, (c % mine + 1) * CW)
                xall[0, CORES * m + core, c // mine, :, at] = jnp.where(
                    covered > 0, embed, seen
                ).astype(jnp.bfloat16)
            init(m).start()
            return carry

        lax.fori_loop(0, micro, one, 0)


    for b in range(CW // LANES):
        gbuf[b, 0:PAD, :] = jnp.zeros((PAD, LANES), jnp.float32)
        gbuf[b, PAD + frames : 2 * PAD + frames, :] = jnp.zeros((PAD, LANES), jnp.float32)

    ring_pass(1)
    load(wctx_hbm, wctx_ref, 2).wait()
    ring_end(0)

    def prepare(a):
        for h in range(half // LANES):
            at = pl.ds(pl.multiple_of(core * half + h * LANES, LANES), LANES)
            block = wv[a, at, 2 * half : 2 * half + LANES]
            kv[a, h] = block.astype(jnp.float32).T[0:32, :]
        ones = jnp.ones((8, width), jnp.bfloat16)
        for c in range(2 * mine):
            at = slice(c * CW, (c + 1) * CW)
            wsum[a, :, at] = jnp.dot(ones, wv[a, :, at], preferred_element_type=jnp.float32)

    prepare(0)

    def piece(a, i, c, j):
        return xall.at[a, i, c, :, pl.ds(j * LANES, LANES)]

    def hop(i, j):
        return remote(
            piece(2, i, core, j),
            piece(0, i, core, j),
            hop_send.at[i, j],
            hop_recv.at[i, j],
            nxt,
            f,
        )

    def swap(a, i, j, c):
        at = piece(a, i, c, j)
        return remote(at, at, swap_send.at[a, i, j], swap_recv.at[a, i, j], s, peer)

    def swap_in(a, i):
        for j in range(sent):
            swap(a, i, j, 1 - core).wait_recv()

    def scatter(i, j):
        return remote(
            xall.at[2, i, core, pl.ds(j * share, share)],
            enc.at[i // CORES, core],
            csend_sem.at[i, j],
            crecv_sem.at[i // CORES, core],
            j,
            f - core + lax.rem(i, CORES),
        )

    def scatter_in(m, c):
        return remote(
            xall.at[2, 0, 0, pl.ds(0, share)],
            enc.at[m, c],
            csend_sem.at[0, 0],
            crecv_sem.at[m, c],
            s,
            peer,
        )

    def row_sum(v):
        return jnp.sum(v, axis=1, keepdims=True)

    def one_utt(i, carry):
        m = i // CORES
        ours = lax.rem(i, CORES) == core

        def layer(a, carry):
            @pl.when((s == 0) & (a == 0) & jnp.logical_not(ours))
            def _():
                init_in(m).wait_recv()

            @pl.when((s > 0) & (a == 0))
            def _():
                for j in range(sent):
                    hop(i, j).wait_recv()
                    swap(0, i, j, core).start()

            @pl.when((i == 0) & (a == 1))
            def _():
                ring_end(1)
                prepare(1)

            def product(c, col):
                at = pl.ds(pl.multiple_of(c * half, CW), half)
                return jnp.dot(
                    xall[a, i, c], wv[a, at, col], preferred_element_type=jnp.float32
                )

            def columns_of(j):
                value = pl.ds(j * CW, CW)
                gate = pl.ds(half + j * CW, CW)
                return value, gate

            def first(j, carry):
                value, gate = columns_of(j)
                part_sum[j, 0] = product(core, value)
                part_sum[j, 1] = product(core, gate)
                return carry

            for j in range(mine):
                first(j, 0)
            def block(c, j):
                return xall[a, i, c, :, j * CW : (j + 1) * CW].astype(jnp.float32)

            total = jnp.zeros((frames, 1), jnp.float32)
            for j in range(mine):
                total = total + row_sum(block(core, j))
            base = total / half
            square = jnp.zeros((frames, 1), jnp.float32)
            for j in range(mine):
                off = block(core, j) - base
                square = square + row_sum(off * off)

            @pl.when((s > 0) | (a > 0))
            def _():
                swap_in(a, i)

            moved = jnp.zeros((frames, CW), jnp.float32)
            far = jnp.zeros((frames, CW), jnp.float32)
            for j in range(mine):
                off = block(1 - core, j) - base
                moved = moved + off
                far = far + off * off
            shift = row_sum(moved) / width
            center = base + shift
            spread = (square + row_sum(far)) / width - shift * shift
            scale = lax.rsqrt(spread + 1e-05)

            def second(j, carry):
                value, gate = columns_of(j)
                v = part_sum[j, 0] + product(1 - core, value)
                v = (v - center * wsum[a, 0:1, value]) * scale
                g = part_sum[j, 1] + product(1 - core, gate)
                g = (g - center * wsum[a, 0:1, gate]) * scale
                glu = (v * jax.nn.sigmoid(g)).astype(jnp.bfloat16).astype(jnp.float32)
                for h in range(CW // LANES):
                    gbuf[h, PAD : PAD + frames, :] = glu[:, h * LANES : (h + 1) * LANES]
                for h in range(CW // LANES):
                    lane = pl.ds(j * CW + h * LANES, LANES)
                    for r in range(0, frames, GROUP):
                        mixed = jnp.zeros((GROUP, LANES), jnp.float32)
                        for k in range(TAPS):
                            taps = kv[a, j * (CW // LANES) + h, k : k + 1, :]
                            mixed = mixed + gbuf[h, r + k + 1 : r + k + 1 + GROUP, :] * taps
                        kept = xall[a, i, core, r : r + GROUP, lane].astype(jnp.float32)
                        xall[a + 1, i, core, r : r + GROUP, lane] = (
                            kept + mixed * jax.nn.sigmoid(mixed)
                        ).astype(jnp.bfloat16)

                    @pl.when(a == 0)
                    def _():
                        swap(1, i, j * (CW // LANES) + h, core).start()

                    @pl.when((a == 1) & (s < last))
                    def _():
                        hop(i, j * (CW // LANES) + h).start()

                return carry

            for j in range(mine):
                second(j, 0)
            return carry

        lax.fori_loop(0, 2, layer, 0)

        @pl.when(s == last)
        def _():
            for j in range(last):
                scatter(i, j).start()

            @pl.when(jnp.logical_not(ours))
            def _():
                scatter(i, last).start()

        return carry

    lax.fori_loop(0, utts, one_utt, 0)

    def score(m, carry):
        @pl.when(s < last)
        def _():
            scatter_in(m, core).wait_recv()

        @pl.when(s == last)
        def _():
            enc[m, core] = xall[2, CORES * m + core, core, last * share : (last + 1) * share, :]

        scatter_in(m, 1 - core).wait_recv()
        ctx = jnp.zeros((share, wctx_ref.shape[1]), jnp.float32)
        for c in range(CORES):
            ctx = ctx + jnp.dot(
                enc[m, c],
                wctx_ref[c * half : (c + 1) * half, :],
                preferred_element_type=jnp.float32,
            )
        ctx = (ctx * lax.rsqrt(row_sum(ctx * ctx) + 1e-06)).astype(jnp.bfloat16)
        spots = lax.broadcasted_iota(jnp.int32, (share, frames), 1)
        rows_at = lax.broadcasted_iota(jnp.int32, (share, frames), 0) + s * share
        sims = 10.0 * lax.dot_general(
            ctx, tgt[m], (((1,), (1,)), ((), ())), preferred_element_type=jnp.float32
        )
        positive = jnp.sum(jnp.where(spots == rows_at, sims, 0.0), axis=1, keepdims=True)
        negative = jnp.sum(cnt[m] * jnp.exp(sims), axis=1, keepdims=True)
        loss = jnp.log(jnp.exp(positive) + negative) - positive
        across_row = lax.broadcasted_iota(jnp.int32, (share, share), 1)
        down_row = lax.broadcasted_iota(jnp.int32, (share, share), 0)
        on_diagonal = jnp.where(across_row == down_row, loss, 0.0)
        out_ref[pl.ds(m, 1), :] = jnp.sum(on_diagonal, axis=0, keepdims=True)
        return carry

    lax.fori_loop(0, micro, score, 0)

    for t in range(2):
        for h in range(CORES):

            @pl.when(jnp.logical_not(stays[t] & (core == h)))
            def _():
                for p in range(3):
                    own_out(t, h, p).wait_send()

    for a in range(2):
        for n in range(7):
            for u in range(CORES):
                ring_out(a, n, u).wait_send()

    @pl.when(s == 0)
    def _():
        for m in range(micro):
            init(m).wait_send()

    def drain(i, carry):
        for j in range(sent):
            swap(1, i, j, core).wait_send()

            @pl.when(s < last)
            def _():
                hop(i, j).wait_send()

            @pl.when(s > 0)
            def _():
                swap(0, i, j, core).wait_send()

        @pl.when(s == last)
        def _():
            for j in range(last):
                scatter(i, j).wait_send()

            @pl.when(lax.rem(i, CORES) != core)
            def _():
                scatter(i, last).wait_send()

        return carry

    lax.fori_loop(0, utts, drain, 0)


def relay(sections, columns, feats, w_in, taps, w_ctx, w_tgt, embed, starts, picks):
    micro, frames, width = feats.shape
    share = frames // sections
    proj = w_ctx.shape[1]
    utts = CORES * micro
    half = width // CORES
    mine = half // CW
    vmem = pl.BlockSpec(memory_space=pltpu.VMEM)
    smem = pl.BlockSpec(memory_space=pltpu.SMEM)
    hbm = pl.BlockSpec(memory_space=pl.ANY)
    dma = pltpu.SemaphoreType.DMA
    bf16 = jnp.bfloat16
    return pl.pallas_call(
        functools.partial(relay_kernel, sections, columns),
        out_shape=jax.ShapeDtypeStruct((micro, share), jnp.float32),
        in_specs=[hbm, hbm, hbm, hbm, hbm, vmem, smem, vmem],
        out_specs=vmem,
        scratch_shapes=[
            pltpu.VMEM(feats.shape, bf16),
            pltpu.VMEM(w_ctx.shape, bf16),
            pltpu.VMEM(w_tgt.shape, bf16),
            dma((3,)),
            pltpu.VMEM((3, utts, CORES, frames, half), bf16),
            pltpu.VMEM((mine, 2, frames, CW), jnp.float32),
            pltpu.VMEM((CW // LANES, frames + 2 * PAD, LANES), jnp.float32),
            pltpu.VMEM((2, 8, 2 * half), jnp.float32),
            pltpu.VMEM((2, width, 2 * half + LANES), bf16),
            pltpu.VMEM((2, half // LANES, 32, LANES), jnp.float32),
            pltpu.VMEM((micro, frames, proj), bf16),
            pltpu.VMEM((micro, share, frames), jnp.float32),
            pltpu.VMEM((micro, CORES, share, half), bf16),
            dma((2, CORES, 3)),
            dma((2, CORES, 3)),
            dma((2, 7, CORES)),
            dma((2, 7, CORES)),
            dma((micro,)),
            dma((micro,)),
            dma((utts, half // LANES)),
            dma((utts, half // LANES)),
            dma((2, utts, half // LANES)),
            dma((2, utts, half // LANES)),
            dma((utts, sections)),
            dma((micro, CORES)),
        ],
        compiler_params=pltpu.CompilerParams(
            collective_id=0, has_side_effects=True, vmem_limit_bytes=60 << 20
        ),
    )(feats, w_in, taps, w_ctx, w_tgt, embed, starts, picks)


def on_device(feats, w_in, dw_kernel, mask_embed, w_ctx, w_tgt, mask_starts, distractors):
    sections = lax.axis_size("section")
    columns = lax.axis_size("fsdp")

    taps = dw_kernel[:, 0].transpose(0, 2, 1)
    taps = jnp.pad(taps, ((0, 0), (0, 0), (0, LANES - taps.shape[2])))
    loss = relay(
        sections,
        columns,
        feats[:, 0],
        w_in[:, 0],
        taps,
        w_ctx,
        w_tgt,
        mask_embed[None, :],
        mask_starts[:, 0],
        distractors[:, 0],
    )
    return loss[:, None, :]


def solution(mesh):
    placed = (
        P(None, "fsdp", None, None),
        P(None, "section", "fsdp", None),
        P(None, "section", None, "fsdp"),
        P(),
        P(),
        P(),
        P(None, "fsdp", None),
        P(None, "fsdp", "section", None),
    )
    return jax.shard_map(
        on_device, mesh=mesh, in_specs=placed, out_specs=P(None, "fsdp", "section"), check_vma=False
    )
```
